32 devices in a mesh: groups: 2 (over y), seq: 4 (over z), chan: 2 (over x), dp: 2 (over core).
Axes of the slice: x: 2, y: 2, z: 4, core: 2. Of those that a mesh axis runs over, the one named last changes fastest.
Arguments:
- signal: bfloat16 [4, 2560, 1536], P(('groups', 'dp'), 'seq', 'chan'), parts along dimension 0, may hold values from -100 to 100
- lengths: int32 [4, 8], P(('groups', 'dp')), parts along dimension 0, may hold values from 1 to 1280, 2560 in all within a row
- dilations: int32 [2], replicated, may hold values from 1 to 64, as said below
- w_conv: bfloat16 [2, 3, 1536, 768], P(None, None, None, 'chan'), may hold values from -0.09375 to 0.09375
- w_proj: bfloat16 [2, 768, 1536], P(None, 'chan'), may hold values from -0.3125 to 0.3125
- gains: float32 [2, 1536], P(None, 'chan'), may hold values from 0.1 to 1.9
- biases: float32 [2, 1536], P(None, 'chan'), may hold values from -3 to 3
Outputs:
- result: bfloat16 [4, 2560, 1536], P(('groups', 'dp'), 'seq', 'chan'), parts along dimension 0
The draws below stay inside these ranges and needn't reach their ends.
There are 2 independent parts, one for each index of `groups`. The reference program is written for one: setup_inputs(seed, part) draws one part's arguments, and reference() takes and returns one part's arrays. A program takes and returns all parts, laid end to end along the dimension named above; an argument that names none is the same for every part. Nothing has to cross between parts.
Inputs may be any that keep to these rules, and one draw needn't show every extreme that they name: `dilations`: exactly one block has dilation 64, the others smaller ones.
All inputs are finite; a program needn't handle non-finite values.
Results may differ from the reference program's by a relative error of at most 0.008.
Values may be sent and summed in bfloat16 or wider, within the bound.
No kernel may reach another device: no remote copies, remote signals or barrier semaphores. Data moves between devices by JAX's collectives and lax.ppermute only.
A program may use at most 64 MiB of HBM per device.

```python
import math
import jax
import jax.numpy as jnp
import numpy as np
from jax import lax

CHANNELS = 1536
INNER = 768
LAYERS = 2
DILATION_MAX = 64
BINS_DEV = 640
BINS = 2560
SEQUENCES = 2
SEGMENTS = 8
N_CHAN = 2


def draw_signal(key, part):
    keys = jax.random.split(key, 3)
    ramp = jnp.exp(math.log(3.0) * (jnp.arange(BINS, dtype=jnp.float32) / BINS - 0.5))[None, :, None]
    base = jnp.clip(jax.random.normal(keys[0], (SEQUENCES, BINS, CHANNELS), jnp.float32), -5.0, 5.0)
    row_scale = jnp.exp(jax.random.uniform(keys[1], (SEQUENCES, BINS, 1), jnp.float32, -1.15, 1.15))
    col_scale = jnp.exp(jax.random.uniform(keys[2], (1, 1, CHANNELS), jnp.float32, -1.15, 1.15))
    values = base * row_scale * col_scale * ramp
    return values.astype(jnp.bfloat16)


def draw_dilations(key, part):
    first, second = jax.random.split(jax.random.fold_in(key, 7))
    chosen = jax.random.randint(first, (LAYERS,), 1, DILATION_MAX, dtype=jnp.int32)
    where_max = jax.random.randint(second, (), 0, LAYERS, dtype=jnp.int32)
    return jnp.where(jnp.arange(LAYERS, dtype=jnp.int32) == where_max, DILATION_MAX, chosen).astype(jnp.int32)


def raised(drawn, stream_key, source, target, parts, factor):
    def block_of(position):
        return (jnp.arange(drawn.shape[position]) // (drawn.shape[position] // parts)).reshape((-1,) + (1,) * (drawn.ndim - 1 - position))

    near = jax.random.permutation(stream_key, parts)[block_of(target)]
    second = (block_of(target) + parts // 2) % parts
    return jnp.where((block_of(source) == near) | (block_of(source) == second), factor * drawn, drawn)


def steps_of(rng, dims, cuts, low, high):
    level = 1.0
    for position, parts in cuts:
        heights = jax.random.uniform(jax.random.fold_in(jax.random.fold_in(rng, 6), position), (parts,), jnp.float32, low / len(cuts), high / len(cuts))
        level = level * jnp.repeat(jnp.exp(heights), dims[position] // parts).reshape((-1,) + (1,) * (len(dims) - 1 - position))
    return level


def profile(amount, total, reach, lean):
    portions = [(1 << 20) // math.isqrt(grade ** lean) + 1 for grade in range(2, amount + 1)]
    surplus, counts = total - reach - (amount - 1), [1] * (amount - 1)
    while surplus > 0:
        candidates = [i for i in range(amount - 1) if counts[i] < reach]
        mass, budget = sum([portions[i] for i in candidates]), surplus
        for i in candidates:
            more = min(reach - counts[i], max(1, budget * portions[i] // mass), surplus)
            counts[i] = counts[i] + more
            surplus = surplus - more
    return np.array([reach] + counts)


def ragged(stream_key, amount, total, bound, skew):
    if amount == 2:
        one = jax.random.randint(stream_key, (), max(1, total - bound), min(bound, total - 1) + 1)
        return jnp.stack([one, total - one])
    sizes = jnp.asarray(profile(amount, total, bound, skew), jnp.int32)
    couples = (amount - 1) // 2
    source_of, sink = sizes[1:1 + 2 * couples:2], sizes[2:2 + 2 * couples:2]
    margin = jnp.minimum(source_of - 1, bound - sink)
    moved = jax.random.randint(jax.random.fold_in(stream_key, 1), (couples,), 0, 1 << 20) % (margin + 1)
    sizes = sizes.at[1:1 + 2 * couples:2].set(source_of - moved).at[2:2 + 2 * couples:2].set(sink + moved)
    return sizes[jax.random.permutation(jax.random.fold_in(stream_key, 2), amount)]


def noise(stream_key, dims, scale, bound, cuts=(), held_as=jnp.bfloat16):
    entries = scale * jax.random.normal(stream_key, dims, jnp.float32)
    if cuts:
        entries = entries * steps_of(stream_key, dims, cuts, -0.22, 0.18)
    return jnp.clip(entries, -bound, bound).astype(held_as)


def bell_draw_with(rng, dims, width, most, pieces, heavy, held_as=jnp.bfloat16):
    values = width * jax.random.normal(rng, dims, jnp.float32)
    if pieces:
        values = values * steps_of(rng, dims, pieces, -0.22, 0.18)
    return jnp.clip(raised(values, jax.random.fold_in(rng, 3), *heavy), -most, most).astype(held_as)


def setup_inputs(seed: int = 0, part: int = 0) -> dict:
    key_list = jax.random.split(jax.random.key(seed), 8)
    part_splits = jax.random.split(jax.random.fold_in(key_list[7], part), 8)
    return {
        "signal": draw_signal(jax.random.fold_in(jax.random.fold_in(key_list[7], part), 71), part),
        "lengths": jax.vmap(lambda own: ragged(own, SEGMENTS, BINS, 2 * BINS_DEV, 2))(jax.random.split(part_splits[1], SEQUENCES)).reshape((SEQUENCES, SEGMENTS)).astype(jnp.int32),
        "dilations": draw_dilations(jax.random.fold_in(key_list[7], 71), part),
        "w_conv": noise(key_list[3], (LAYERS, 3, CHANNELS, INNER), (3 * CHANNELS) ** -0.5, 0.09375, ((3, 2),)),
        "w_proj": bell_draw_with(key_list[4], (LAYERS, INNER, CHANNELS), INNER ** -0.5, 0.3125, ((1, 2),), (1, 2, 2, 2.0)),
        "gains": jnp.clip(1.0 + 0.18 * jax.random.normal(key_list[5], (LAYERS, CHANNELS), jnp.float32), 0.1, 1.9),
        "biases": noise(key_list[6], (LAYERS, CHANNELS), 0.5, 3.0, ((1, 2),), jnp.float32),
    }


eps = 1e-05
far_away = 1 << 30

def segment_bounds(lengths, places):
    ends = jnp.cumsum(lengths, axis=-1, dtype=jnp.int32)
    starts = ends - lengths
    low = lax.optimization_barrier(jnp.max(jnp.where(starts[:, None, :] <= places[None, :, None], starts[:, None, :], -far_away), axis=-1))
    high = lax.optimization_barrier(jnp.min(jnp.where(ends[:, None, :] > places[None, :, None], ends[:, None, :], far_away), axis=-1))
    return (low, high)

def norm_act(state, gain, bias):
    values = state.astype(jnp.float32)
    mean = lax.optimization_barrier(jnp.mean(values, axis=(0, 1)))
    spread = lax.optimization_barrier(jnp.mean(jnp.square(values - mean), axis=(0, 1)))
    return jax.nn.gelu((values - mean) * lax.rsqrt(spread + eps) * gain + bias).astype(jnp.bfloat16)

def reference(signal, lengths, dilations, w_conv, w_proj, gains, biases):
    places = jnp.arange(BINS, dtype=jnp.int32)
    low, high = segment_bounds(lengths, places)
    zero = jnp.zeros((), jnp.bfloat16)
    state = signal
    share = INNER // N_CHAN
    for layer in range(LAYERS):
        dilation = dilations[layer].astype(jnp.int32)
        normed = norm_act(state, gains[layer], biases[layer])
        padded = jnp.pad(normed, ((0, 0), (DILATION_MAX, DILATION_MAX), (0, 0)))
        left = lax.dynamic_slice_in_dim(padded, (DILATION_MAX - dilation).astype(jnp.int32), BINS, axis=1)
        right = lax.dynamic_slice_in_dim(padded, (DILATION_MAX + dilation).astype(jnp.int32), BINS, axis=1)
        left = jnp.where((places - dilation >= low)[:, :, None], left, zero)
        right = jnp.where((places + dilation < high)[:, :, None], right, zero)
        taps = jnp.concatenate([left, normed, right], axis=2).reshape(SEQUENCES * BINS, 3 * CHANNELS)
        mixed = jnp.dot(taps, w_conv[layer].reshape(3 * CHANNELS, INNER), preferred_element_type=jnp.float32)
        inner = jax.nn.gelu(mixed).astype(jnp.bfloat16)
        update = jnp.zeros((SEQUENCES * BINS, CHANNELS), jnp.float32)
        for block in range(N_CHAN):
            partial_sum = jnp.dot(inner[:, block * share:(block + 1) * share], w_proj[layer][block * share:(block + 1) * share], preferred_element_type=jnp.float32).astype(jnp.bfloat16)
            update = update + lax.optimization_barrier(partial_sum).astype(jnp.float32)
        state = (state.astype(jnp.float32) + update.reshape(SEQUENCES, BINS, CHANNELS)).astype(jnp.bfloat16)
    return state
```

```python
import functools

import jax
import jax.numpy as jnp
from jax import lax
from jax.experimental import pallas as pl
from jax.experimental.pallas import tpu as pltpu
from jax.sharding import PartitionSpec as P

LAYERS = 2
HALO = 64
EPS = 1e-05
F32 = jnp.float32
BF16 = jnp.bfloat16
SWAP = [(0, 1), (1, 0)]
VMEM_LIMIT = 24 << 20


def gelu(x):
    return jax.nn.gelu(x)


def merged(a, b, n):
    gap = a[0] - b[0]
    return jnp.stack([(a[0] + b[0]) * 0.5, a[1] + b[1] + gap * gap * (0.5 * n)])


def batch_stats(local, n):
    total = local
    for axis in ("dp", "seq"):
        size = lax.axis_size(axis)
        step = 1
        while step < size:
            pairs = [(i, i ^ step) for i in range(size)]
            total = merged(total, lax.ppermute(total, axis, pairs), n)
            n *= 2
            step *= 2
    return total[0], total[1] / n


def conv_kernel(pieces, layer, rows, first, n_src, sc, stats, keep_l, keep_r, w_hbm, *rest):
    srcs, (out, xbuf, nbuf, wbuf, p0, p2, sems, wsems) = rest[:n_src], rest[n_src:]
    copies = []
    for tap in range(3):
        copies.append(pltpu.make_async_copy(w_hbm.at[layer, tap], wbuf.at[tap], wsems.at[tap]))
        copies[-1].start()
    moves = []
    for k, (src, at, count, to, half) in enumerate(pieces):
        moves.append(start_piece(srcs[src], at, count, to, half, sc, xbuf, sems.at[k]))
    for m in moves:
        m.wait()
    ext = rows + 2 * HALO
    block = 32
    mean = stats[0:1, :]
    scale = stats[1:2, :]
    bias = stats[2:3, :]

    @pl.loop(0, ext // block)
    def _(i):
        at = pl.ds(pl.multiple_of(i * block, block), block)
        v = xbuf[at, :].astype(F32)
        nbuf[at, :] = gelu((v - mean) * scale + bias).astype(BF16)

    dot = functools.partial(jnp.dot, preferred_element_type=F32)
    copies[0].wait()
    p0[0 : rows + HALO, :] = dot(nbuf[0 : rows + HALO, :], wbuf[0])
    copies[2].wait()
    p2[0 : rows + HALO, :] = dot(nbuf[HALO:ext, :], wbuf[2])
    copies[1].wait()
    mid = dot(nbuf[HALO : HALO + rows, :], wbuf[1])
    d = sc[layer]
    width = out.shape[1]
    for r in range(0, rows, HALO):
        left = shifted(p0, r + HALO - d, HALO)
        right = shifted(p2, r + d, HALO)
        here = slice(first + r, first + r + HALO)
        for c in range(0, width, 128):
            wide = min(128, width - c)
            cs = slice(c, c + wide)
            kl, kr = keep_l[here, :wide] > 0, keep_r[here, :wide] > 0
            mixed = jnp.where(kl, left[:, cs], 0.0) + jnp.where(kr, right[:, cs], 0.0)
            out[r : r + HALO, cs] = gelu(mid[r : r + HALO, cs] + mixed).astype(BF16)


def shifted(ref, start, count):
    base = pl.multiple_of((start // 8) * 8, 8)
    tall = ref[pl.ds(base, count + 8), :]
    return pltpu.roll(tall, (count + 8 - (start - base)) % (count + 8), 0)[:count]


def side_of(sc, back):
    return lax.rem(sc[2] - back + sc[4], sc[4])


def start_piece(src, at, count, to, back, sc, buf, sem):
    if back is None:
        dst = buf.at[pl.ds(to, count), :]
    else:
        width = src.shape[1]
        at_col = pl.multiple_of(side_of(sc, back) * width, 128)
        dst = buf.at[pl.ds(to, count), pl.ds(at_col, width)]
    copy = pltpu.make_async_copy(src.at[pl.ds(at, count), :], dst, sem)
    copy.start()
    return copy


def start_weights(layer, cols, n, sc, w_hbm, wa, wb, wbuf, sems):
    part = wa[0].shape[0]
    copies = [pltpu.make_async_copy(w_hbm.at[layer, :, cols], wbuf.at[0], sems.at[0])]
    for k in range(1, n):
        for j, (src, core) in enumerate(((wa[k - 1], sc[3]), (wb[k - 1], 1 - sc[3]))):
            dst = wbuf.at[k, pl.ds(pl.multiple_of(core * part, 16), part), :]
            copies.append(pltpu.make_async_copy(src, dst, sems.at[2 * k - 1 + j]))
    for c in copies:
        c.start()
    return copies


def update_of(inners, wbuf, cols):
    total = None
    for k, inner in enumerate(inners):
        term = jnp.dot(inner[...], wbuf[k, :, cols], preferred_element_type=F32)
        term = term.astype(BF16).astype(F32)
        total = term if total is None else total + term
    return total


ANY = pl.BlockSpec(memory_space=pl.ANY)
INV = pl.BlockSpec(memory_space=pltpu.VMEM)
INS = pl.BlockSpec(memory_space=pltpu.SMEM)


def conv(pieces, srcs, layer, rows, first, sc, stats, keep, w_conv):
    channels, width = w_conv.shape[2:]
    ext = rows + 2 * HALO
    return pl.pallas_call(
        functools.partial(conv_kernel, pieces, layer, rows, first, len(srcs)),
        out_shape=jax.ShapeDtypeStruct((rows, width), BF16),
        in_specs=[INS, INV, INV, INV, ANY] + [ANY] * len(srcs),
        out_specs=INV,
        scratch_shapes=[
            pltpu.VMEM((ext, channels), BF16),
            pltpu.VMEM((ext, channels), BF16),
            pltpu.VMEM((3, channels, width), BF16),
            pltpu.VMEM((rows + HALO + 8, width), F32),
            pltpu.VMEM((rows + HALO + 8, width), F32),
            pltpu.SemaphoreType.DMA((len(pieces),)),
            pltpu.SemaphoreType.DMA((3,)),
        ],
        compiler_params=pltpu.CompilerParams(vmem_limit_bytes=VMEM_LIMIT),
        name=f"conv{layer}",
    )(sc, stats, keep[0], keep[1], w_conv, *srcs)


def proj0_kernel(pieces, rows, n, n_src, sc, *rest):
    inners, rest = rest[:n], rest[n:]
    w_hbm, wa, wb, rest = rest[0], rest[1:n], rest[n : 2 * n - 1], rest[2 * n - 1 :]
    srcs, (out, stat, xbuf, wbuf, sems, wsems) = rest[:n_src], rest[n_src:]
    copies = start_weights(0, slice(None), n, sc, w_hbm, wa, wb, wbuf, wsems)
    for k, (src, at, count, to, back) in enumerate(pieces):
        copies.append(start_piece(srcs[src], at, count, to, back, sc, xbuf, sems.at[k]))
    for c in copies:
        c.wait()
    for col in range(0, out.shape[1], 256):
        cs = slice(col, col + 256)
        new = (xbuf[:, cs].astype(F32) + update_of(inners, wbuf, cs)).astype(BF16)
        out[:, cs] = new
        v = new.astype(F32)
        pivot = jnp.mean(v[0:8], axis=0, keepdims=True)
        gap = v - pivot
        s1 = jnp.sum(gap, axis=0, keepdims=True)
        s2 = jnp.sum(gap * gap, axis=0, keepdims=True)
        off = s1 * (1.0 / rows)
        stat[0:1, cs] = pivot + off
        stat[1:2, cs] = s2 - s1 * off


def proj0(pieces, srcs, rows, sc, inners, w_proj, wa, wb):
    hidden, channels = w_proj.shape[1:]
    n = len(inners)
    return pl.pallas_call(
        functools.partial(proj0_kernel, pieces, rows, n, len(srcs)),
        out_shape=(
            jax.ShapeDtypeStruct((rows, channels), BF16),
            jax.ShapeDtypeStruct((2, channels), F32),
        ),
        in_specs=[INS] + [INV] * n + [ANY] * (2 * n - 1 + len(srcs)),
        out_specs=(INV, INV),
        scratch_shapes=[
            pltpu.VMEM((rows, channels), BF16),
            pltpu.VMEM((n, hidden, channels), BF16),
            pltpu.SemaphoreType.DMA((len(pieces),)),
            pltpu.SemaphoreType.DMA((2 * n - 1,)),
        ],
        compiler_params=pltpu.CompilerParams(vmem_limit_bytes=VMEM_LIMIT),
        name="proj0",
    )(sc, *inners, w_proj, *wa, *wb, *srcs)


def proj1_kernel(n, sc, *rest):
    inners, rest = rest[:n], rest[n:]
    w_hbm, wa, wb, rest = rest[0], rest[1:n], rest[n : 2 * n - 1], rest[2 * n - 1 :]
    state, out, xbuf, wbuf, sem, wsems = rest
    width = out.shape[1]
    cols = pl.ds(pl.multiple_of(sc[2] * width, 128), width)
    copies = start_weights(1, cols, n, sc, w_hbm, wa, wb, wbuf, wsems)
    copies.append(pltpu.make_async_copy(state.at[:, cols], xbuf, sem))
    copies[-1].start()
    for c in copies:
        c.wait()
    for col in range(0, width, 128):
        cs = slice(col, col + 128)
        out[:, cs] = (xbuf[:, cs].astype(F32) + update_of(inners, wbuf, cs)).astype(BF16)


def proj1(rows, sc, inners, w_proj, wa, wb, state):
    hidden, channels = w_proj.shape[1:]
    n = len(inners)
    width = channels // n
    return pl.pallas_call(
        functools.partial(proj1_kernel, n),
        out_shape=jax.ShapeDtypeStruct((rows, width), BF16),
        in_specs=[INS] + [INV] * n + [ANY] * (2 * n),
        out_specs=INV,
        scratch_shapes=[
            pltpu.VMEM((rows, width), BF16),
            pltpu.VMEM((n, hidden, width), BF16),
            pltpu.SemaphoreType.DMA,
            pltpu.SemaphoreType.DMA((2 * n - 1,)),
        ],
        compiler_params=pltpu.CompilerParams(vmem_limit_bytes=VMEM_LIMIT),
        name="proj1",
    )(sc, *inners, w_proj, *wa, *wb, state)


def keeps(lengths, places, dilation):
    ends = jnp.cumsum(lengths, dtype=jnp.int32)
    left = jnp.zeros(places.shape, jnp.bool_)
    right = jnp.zeros(places.shape, jnp.bool_)
    for k in range(lengths.shape[0]):
        start, end = ends[k] - lengths[k], ends[k]
        left |= (places - dilation < start) & (start <= places)
        right |= (places < end) & (end <= places + dilation)
    return jnp.where(left, 0.0, 1.0).astype(F32), jnp.where(right, 0.0, 1.0).astype(F32)


def on_device(signal, lengths, dilations, w_conv, w_proj, gains, biases):
    own = signal[0]
    rows, width = own.shape
    half = rows // 2
    chan, core, place = lax.axis_index("chan"), lax.axis_index("dp"), lax.axis_index("seq")
    n_seq, n = lax.axis_size("seq"), lax.axis_size("chan")
    up = [(i, i + 1) for i in range(n_seq - 1)]
    down = [(i + 1, i) for i in range(n_seq - 1)]
    perm = lax.ppermute
    sc = jnp.concatenate([dilations, jnp.stack([chan, core, jnp.int32(n)]).astype(jnp.int32)])

    def others(value):
        return [perm(value, "chan", [(i, (i + k) % n) for i in range(n)]) for k in range(1, n)]

    def true_order(mine, other):
        parts = [mine] + list(other)
        if n == 2:
            first = jnp.where(chan == 0, parts[0], parts[1])
            return jnp.concatenate([first, jnp.where(chan == 0, parts[1], parts[0])], axis=-1)
        stack = jnp.take(jnp.stack(parts), (chan - jnp.arange(n)) % n, axis=0)
        return jnp.concatenate([stack[k] for k in range(n)], axis=-1)

    edges = others(jnp.concatenate([own[:HALO], own[rows - HALO :]]))
    cut = half + HALO
    end = rows - HALO
    rest_a = others(own[HALO:cut])
    rest_b = others(own[cut:end])
    low0 = perm(true_order(own[end:], [e[HALO:] for e in edges]), "seq", up)
    high0 = perm(true_order(own[:HALO], [e[:HALO] for e in edges]), "seq", down)

    part = w_proj.shape[1] // 2
    mine0 = lax.dynamic_slice(w_proj, (0, core * part, 0), (1, part, n * width))[0]
    wa0 = others(mine0)
    wb0 = [perm(w, "dp", SWAP) for w in wa0]
    wa1 = []
    for k in range(1, n):
        at = (1, core * part, (chan + k) % n * width)
        mine1 = lax.dynamic_slice(w_proj, at, (1, part, width))[0]
        wa1.append(perm(mine1, "chan", [(i, (i + k) % n) for i in range(n)]))
    wb1 = [perm(w, "dp", SWAP) for w in wa1]

    values = own.astype(F32)
    mean = jnp.mean(values, axis=0)
    local = jnp.stack([mean, jnp.sum(jnp.square(values - mean), axis=0)])
    mean, var = batch_stats(local, rows)
    mine = jnp.stack([mean, lax.rsqrt(var + EPS) * gains[0], biases[0], gains[1], biases[1]])
    vecs = true_order(mine, others(mine))

    places = place * rows + lax.broadcasted_iota(jnp.int32, (rows, 128), 0)
    keep = [keeps(lengths[0], places, dilations[layer]) for layer in range(LAYERS)]

    srcs = (own, low0, high0, *edges, *rest_a, *rest_b)
    behind = [(k, 2 + k, 1 + n + k, 2 * n + k) for k in range(1, n)]
    pieces_a = [(1, 0, HALO, 0, None), (0, 0, cut, HALO, 0)]
    pieces_b = [(0, half - HALO, half + HALO, 0, 0), (2, 0, HALO, half + HALO, None)]
    res_a, res_b = [(0, 0, half, 0, 0)], [(0, half, half, 0, 0)]
    for k, e, a, b in behind:
        pieces_a += [(e, 0, HALO, HALO, k), (a, 0, cut - HALO, 2 * HALO, k)]
        pieces_b += [
            (a, half - 2 * HALO, 2 * HALO, 0, k),
            (b, 0, end - cut, 2 * HALO, k),
            (e, HALO, HALO, 2 * HALO + end - cut, k),
        ]
        res_a += [(e, 0, HALO, 0, k), (a, 0, half - HALO, HALO, k)]
        res_b += [
            (a, half - HALO, HALO, 0, k),
            (b, 0, end - cut, HALO, k),
            (e, HALO, HALO, HALO + end - cut, k),
        ]
    early = srcs[: 1 + 2 * n]
    inner_a = conv(pieces_a, early, 0, half, 0, sc, vecs[:3], keep[0], w_conv)
    inner_b = conv(pieces_b, srcs, 0, half, half, sc, vecs[:3], keep[0], w_conv)
    inners_a = [inner_a] + others(inner_a)
    inners_b = [inner_b] + others(inner_b)
    state_a, stat_a = proj0(res_a, early, half, sc, inners_a, w_proj, wa0, wb0)
    state_b, stat_b = proj0(res_b, srcs, half, sc, inners_b, w_proj, wa0, wb0)
    high1 = perm(state_a[:HALO], "seq", down)
    low1 = perm(state_b[half - HALO :], "seq", up)

    mean, var = batch_stats(merged(stat_a, stat_b, half), rows)
    vecs1 = jnp.stack([mean, lax.rsqrt(var + EPS) * vecs[3], vecs[4]])

    srcs = (state_a, state_b, low1, high1)
    pieces_a = ((2, 0, HALO, 0, None), (0, 0, half, HALO, None), (1, 0, HALO, half + HALO, None))
    pieces_b = (
        (0, half - HALO, HALO, 0, None),
        (1, 0, half, HALO, None),
        (3, 0, HALO, half + HALO, None),
    )
    inner_a = conv(pieces_a, srcs, 1, half, 0, sc, vecs1, keep[1], w_conv)
    inner_b = conv(pieces_b, srcs, 1, half, half, sc, vecs1, keep[1], w_conv)
    inners_a = [inner_a] + others(inner_a)
    inners_b = [inner_b] + others(inner_b)
    out_a = proj1(half, sc, inners_a, w_proj, wa1, wb1, state_a)
    out_b = proj1(half, sc, inners_b, w_proj, wa1, wb1, state_b)
    return jnp.concatenate([out_a, out_b])[None]


def solution(mesh):
    placed = (
        P(("groups", "dp"), "seq", "chan"),
        P(("groups", "dp"), None),
        P(),
        P(None, None, None, "chan"),
        P(None, "chan", None),
        P(None, "chan"),
        P(None, "chan"),
    )
    return jax.shard_map(
        on_device,
        mesh=mesh,
        in_specs=placed,
        out_specs=P(("groups", "dp"), "seq", "chan"),
        check_vma=False,
    )
```

```python
import functools

import jax
import jax.numpy as jnp
from jax import lax
from jax.experimental import pallas as pl
from jax.experimental.pallas import tpu as pltpu
from jax.sharding import PartitionSpec as P

HALO = 64
EPS = 1e-05
F32 = jnp.float32
BF16 = jnp.bfloat16
SWAP = [(0, 1), (1, 0)]
VMEM_LIMIT = 24 << 20

ANY = pl.BlockSpec(memory_space=pl.ANY)
HBM = pl.BlockSpec(memory_space=pltpu.HBM)
INV = pl.BlockSpec(memory_space=pltpu.VMEM)
INS = pl.BlockSpec(memory_space=pltpu.SMEM)
PARAMS = pltpu.CompilerParams(vmem_limit_bytes=VMEM_LIMIT)
dot = functools.partial(jnp.dot, preferred_element_type=F32)
copy = pltpu.make_async_copy


def shape(dims, dtype):
    return jax.ShapeDtypeStruct(tuple(dims), dtype)


def gelu(x):
    return jax.nn.gelu(x)


def side_of(back, n):
    return lax.rem(lax.axis_index("chan") - back + n, n)


def columns(back, n, width):
    return pl.ds(pl.multiple_of(side_of(back, n) * width, 128), width)


def run(copies):
    for c in copies:
        c.start()
    for c in copies:
        c.wait()


def sums_about(v, pivot):
    gap = (v - pivot).reshape(v.shape[0] // 8, 8, v.shape[1])
    return jnp.sum(gap, axis=0), jnp.sum(gap * gap, axis=0)


def spread_of(pivot, s1, s2, rows):
    s1 = jnp.sum(s1, axis=0, keepdims=True)
    s2 = jnp.sum(s2, axis=0, keepdims=True)
    off = s1 * (1.0 / rows)
    return pivot + off, s2 - s1 * off


def merged(a, b, n):
    gap = a[0:1] - b[0:1]
    return (a[0:1] + b[0:1]) * 0.5, a[1:2] + b[1:2] + gap * gap * (0.5 * n)


def pre_kernel(cut, own, w, gains, biases, sums, edges, rest_a, rest_b, wsend, xbuf, sems):
    rows = own.shape[0]
    end = rows - HALO
    part = wsend.shape[0]
    quarter = lax.axis_index("groups") * 2 + lax.axis_index("dp")
    load = copy(own, xbuf, sems.at[0])
    load.start()
    moves = [
        copy(own.at[pl.ds(0, HALO)], edges.at[pl.ds(0, HALO)], sems.at[1]),
        copy(own.at[pl.ds(end, HALO)], edges.at[pl.ds(HALO, HALO)], sems.at[2]),
        copy(own.at[pl.ds(HALO, cut - HALO)], rest_a, sems.at[3]),
        copy(own.at[pl.ds(cut, end - cut)], rest_b, sems.at[4]),
        copy(w.at[0, pl.ds(pl.multiple_of(quarter * part, 16), part)], wsend, sems.at[5]),
    ]
    for m in moves:
        m.start()
    load.wait()
    pivot = jnp.mean(xbuf[0:16, :].astype(F32)[0:8], axis=0, keepdims=True)
    s1 = s2 = jnp.zeros((8, xbuf.shape[1]), F32)
    for r in range(0, rows, 64):
        t1, t2 = sums_about(xbuf[r : r + 64, :].astype(F32), pivot)
        s1, s2 = s1 + t1, s2 + t2
    mean, m2 = spread_of(pivot, s1, s2, rows)
    sums[0:1, :] = mean
    sums[1:2, :] = m2
    for layer in range(2):
        sums[2 + 2 * layer : 3 + 2 * layer, :] = gains[layer : layer + 1, :]
        sums[3 + 2 * layer : 4 + 2 * layer, :] = biases[layer : layer + 1, :]
    for m in moves:
        m.wait()


def pre(own, w_proj, gains, biases, cut):
    rows, width = own.shape
    part = w_proj.shape[1] // 4
    return pl.pallas_call(
        functools.partial(pre_kernel, cut),
        out_shape=(
            shape((8, width), F32),
            shape((2 * HALO, width), BF16),
            shape((cut - HALO, width), BF16),
            shape((rows - HALO - cut, width), BF16),
            shape((part, w_proj.shape[2]), BF16),
        ),
        in_specs=[HBM, HBM, INV, INV],
        out_specs=(INV, ANY, ANY, ANY, ANY),
        scratch_shapes=[pltpu.VMEM((rows, width), BF16), pltpu.SemaphoreType.DMA((6,))],
        compiler_params=PARAMS,
        name="pre",
    )(own, w_proj, gains, biases)


def join_kernel(n, *refs):
    parts, (stat, joined) = refs[:n], refs[n:]
    for k, part in enumerate(parts):
        cols = columns(k, n, part.shape[1])
        stat[:, cols] = part[0:2, :]
        joined[:, cols] = part[...]


def join(parts):
    n, width = len(parts), parts[0].shape[1]
    return pl.pallas_call(
        functools.partial(join_kernel, n),
        out_shape=(shape((2, n * width), F32), shape((8, n * width), F32)),
        in_specs=[INV] * n,
        out_specs=(INV, INV),
        compiler_params=PARAMS,
        name="join",
    )(*parts)


def merge_kernel(n, a, b, out):
    out[0:1, :], out[1:2, :] = merged(a[...], b[...], n)


def finish_kernel(n, layer, a, b, joined, out):
    mean, m2 = merged(a[...], b[...], n)
    out[0:1, :] = mean
    scale = lax.rsqrt(m2 * (1.0 / (2 * n)) + EPS)
    out[1:2, :] = scale * joined[2 + 2 * layer : 3 + 2 * layer, :]
    out[2:3, :] = joined[3 + 2 * layer : 4 + 2 * layer, :]


def batch_stats(stat, n, joined, layer):
    steps = []
    for axis in ("dp", "seq"):
        size, step = lax.axis_size(axis), 1
        while step < size:
            steps.append((axis, [(i, i ^ step) for i in range(size)]))
            step *= 2
    channels = stat.shape[1]
    for at, (axis, pairs) in enumerate(steps):
        other = lax.ppermute(stat, axis, pairs)
        if at < len(steps) - 1:
            stat = pl.pallas_call(
                functools.partial(merge_kernel, n),
                out_shape=shape((2, channels), F32),
                in_specs=[INV, INV],
                out_specs=INV,
                name="merge",
            )(stat, other)
        else:
            stat = pl.pallas_call(
                functools.partial(finish_kernel, n, layer),
                out_shape=shape((8, channels), F32),
                in_specs=[INV, INV, INV],
                out_specs=INV,
                name="finish",
            )(stat, other, joined)
        n *= 2
    return stat


def edge_kernel(n, own, *rest):
    edges, (low, high, sems) = rest[: n - 1], rest[n - 1 :]
    end = own.shape[0] - HALO
    width = own.shape[1]
    copies = []
    for k in range(n):
        cols = columns(k, n, width)
        first = own.at[pl.ds(0, HALO)] if k == 0 else edges[k - 1].at[pl.ds(0, HALO)]
        last = own.at[pl.ds(end, HALO)] if k == 0 else edges[k - 1].at[pl.ds(HALO, HALO)]
        copies.append(copy(last, low.at[:, cols], sems.at[2 * k]))
        copies.append(copy(first, high.at[:, cols], sems.at[2 * k + 1]))
    run(copies)


def edge_rows(own, edges):
    n = 1 + len(edges)
    return pl.pallas_call(
        functools.partial(edge_kernel, n),
        out_shape=(shape((HALO, n * own.shape[1]), BF16),) * 2,
        in_specs=[HBM] + [ANY] * (n - 1),
        out_specs=(ANY, ANY),
        scratch_shapes=[pltpu.SemaphoreType.DMA((2 * n,))],
        name="edge_rows",
    )(own, *edges)


def keep_kernel(lengths, dilations, out):
    rows = out.shape[1]
    first = lax.axis_index("seq") * rows
    count = lengths.shape[1]

    @pl.loop(0, rows // 64)
    def _(i):
        at = pl.multiple_of(i * 64, 64)
        place = first + at + lax.broadcasted_iota(jnp.int32, (64, 128), 0)

        def step(k, carry):
            start, keep = carry[0], list(carry[1:])
            end = start + lengths[0, k]
            for layer in range(2):
                d = dilations[layer]
                cut_l = (place - d < start) & (start <= place)
                cut_r = (place < end) & (end <= place + d)
                keep[2 * layer] = jnp.where(cut_l, 0.0, keep[2 * layer])
                keep[2 * layer + 1] = jnp.where(cut_r, 0.0, keep[2 * layer + 1])
            return (end, *keep)

        ones = jnp.ones((64, 128), F32)
        done = lax.fori_loop(0, count, step, (jnp.int32(0), ones, ones, ones, ones))
        for k in range(4):
            out[k, pl.ds(at, 64), :] = done[1 + k]


def keeps(lengths, dilations, rows):
    return pl.pallas_call(
        keep_kernel,
        out_shape=shape((4, rows, 128), F32),
        in_specs=[INS, INS],
        out_specs=INV,
        name="keeps",
    )(lengths, dilations)


def shifted(ref, start, count):
    base = pl.multiple_of((start // 8) * 8, 8)
    tall = ref[pl.ds(base, count + 8), :]
    return pltpu.roll(tall, (count + 8 - (start - base)) % (count + 8), 0)[:count]


def piece(src, at, count, to, back, n, buf, sem):
    if back is None:
        dst = buf.at[pl.ds(to, count), :]
    else:
        dst = buf.at[pl.ds(to, count), columns(back, n, src.shape[1])]
    return copy(src.at[pl.ds(at, count), :], dst, sem)


def conv_kernel(pieces, layer, rows, first, n, n_src, dilations, stats, keep, w_hbm, *rest):
    srcs, (out, xbuf, nbuf, wbuf, p0, p2, sems, wsems) = rest[:n_src], rest[n_src:]
    moves = [piece(srcs[p[0]], *p[1:], n, xbuf, sems.at[k]) for k, p in enumerate(pieces)]
    for m in moves:
        m.start()
    weights = [copy(w_hbm.at[layer, tap], wbuf.at[tap], wsems.at[tap]) for tap in range(3)]
    for w in weights:
        w.start()
    for m in moves:
        m.wait()
    ext = rows + 2 * HALO
    block = 16
    mean, scale, bias = stats[0:1, :], stats[1:2, :], stats[2:3, :]

    @pl.loop(0, ext // block)
    def _(i):
        at = pl.ds(pl.multiple_of(i * block, block), block)
        v = xbuf[at, :].astype(F32)
        nbuf[at, :] = gelu((v - mean) * scale + bias).astype(BF16)

    weights[0].wait()
    p0[0 : rows + HALO, :] = dot(nbuf[0 : rows + HALO, :], wbuf[0])
    weights[2].wait()
    p2[0 : rows + HALO, :] = dot(nbuf[HALO:ext, :], wbuf[2])
    weights[1].wait()
    mid = dot(nbuf[HALO : HALO + rows, :], wbuf[1])
    d = dilations[layer]
    width = out.shape[1]
    for r in range(0, rows, HALO):
        left = shifted(p0, r + HALO - d, HALO)
        right = shifted(p2, r + d, HALO)
        here = slice(first + r, first + r + HALO)
        for c in range(0, width, 128):
            wide = min(128, width - c)
            cs = slice(c, c + wide)
            kl, kr = keep[2 * layer, here, :wide] > 0, keep[2 * layer + 1, here, :wide] > 0
            mixed = jnp.where(kl, left[:, cs], 0.0) + jnp.where(kr, right[:, cs], 0.0)
            out[r : r + HALO, cs] = gelu(mid[r : r + HALO, cs] + mixed).astype(BF16)


def conv(pieces, srcs, n, layer, rows, first, dilations, stats, keep, w_conv):
    channels, width = w_conv.shape[2:]
    ext = rows + 2 * HALO
    return pl.pallas_call(
        functools.partial(conv_kernel, pieces, layer, rows, first, n, len(srcs)),
        out_shape=shape((rows, width), BF16),
        in_specs=[INS, INV, INV, HBM] + [ANY] * len(srcs),
        out_specs=INV,
        scratch_shapes=[
            pltpu.VMEM((ext, channels), BF16),
            pltpu.VMEM((ext, channels), BF16),
            pltpu.VMEM((3, channels, width), BF16),
            pltpu.VMEM((rows + HALO + 8, width), F32),
            pltpu.VMEM((rows + HALO + 8, width), F32),
            pltpu.SemaphoreType.DMA((len(pieces),)),
            pltpu.SemaphoreType.DMA((3,)),
        ],
        compiler_params=PARAMS,
        name=f"conv{layer}_{first}",
    )(dilations, stats, keep, w_conv, *srcs)


def weight_copies(layer, cols, w_hbm, sends, wbuf, sems):
    copies = [copy(w_hbm.at[layer, :, cols], wbuf.at[0], sems.at[0])]
    for k, parts in enumerate(sends):
        size = parts[0][0].shape[0]
        for src, at in parts:
            dst = wbuf.at[k + 1, pl.ds(pl.multiple_of(at * size, 16), size), :]
            copies.append(copy(src, dst, sems.at[len(copies)]))
    return copies


def quarters(refs):
    group, core = lax.axis_index("groups"), lax.axis_index("dp")
    ats = (2 * group + core, 2 * (1 - group) + core, 2 * group + 1 - core, 3 - 2 * group - core)
    return [list(zip(refs[i : i + 4], ats)) for i in range(0, len(refs), 4)]


def halves(refs):
    core = lax.axis_index("dp")
    return [list(zip(refs[i : i + 2], (core, 1 - core))) for i in range(0, len(refs), 2)]


def update_of(inners, wbuf, cols):
    total = None
    for k, inner in enumerate(inners):
        term = dot(inner[...], wbuf[k, :, cols]).astype(BF16).astype(F32)
        total = term if total is None else total + term
    return total


def proj0_kernel(pieces, rows, n, n_src, last, *rest):
    inners, w_hbm, sends, rest = rest[:n], rest[n], rest[n + 1 : 5 * n - 3], rest[5 * n - 3 :]
    srcs, rest = rest[:n_src], rest[n_src:]
    if last:
        before, out, stat, edge, xbuf, wbuf, sems, wsems = rest
        wsend = ()
    else:
        out, stat, edge, *wsend, xbuf, wbuf, sems, wsems, ssems = rest
    copies = weight_copies(0, slice(None), w_hbm, quarters(sends), wbuf, wsems)
    copies += [piece(srcs[p[0]], *p[1:], n, xbuf, sems.at[k]) for k, p in enumerate(pieces)]
    moves = []
    for k, dst in enumerate(wsend):
        size, width = dst.shape
        ahead = lax.rem(lax.axis_index("chan") + k + 1, n) * width
        part = pl.ds(pl.multiple_of(lax.axis_index("dp") * size, 16), size)
        src = w_hbm.at[1, part, pl.ds(pl.multiple_of(ahead, 128), width)]
        moves.append(copy(src, dst, ssems.at[k]))
    for c in copies + moves:
        c.start()
    for c in copies:
        c.wait()
    for col in range(0, out.shape[1], 256):
        cs = slice(col, col + 256)
        new = (xbuf[:, cs].astype(F32) + update_of(inners, wbuf, cs)).astype(BF16)
        out[:, cs] = new
        edge[:, cs] = new[rows - HALO :] if last else new[:HALO]
        v = new.astype(F32)
        pivot = jnp.mean(v[0:8], axis=0, keepdims=True)
        mean, m2 = spread_of(pivot, *sums_about(v, pivot), rows)
        if last:
            mean, m2 = merged(before[:, cs], jnp.concatenate([mean, m2]), rows)
        stat[0:1, cs] = mean
        stat[1:2, cs] = m2
    for m in moves:
        m.wait()


def proj0(pieces, srcs, rows, inners, w_proj, sends, before=None):
    hidden, channels = w_proj.shape[1:]
    n = len(inners)
    last = before is not None
    n_send = 0 if last else n - 1
    outs = [shape((rows, channels), BF16), shape((2, channels), F32), shape((HALO, channels), BF16)]
    outs += [shape((hidden // 2, channels // n), BF16)] * n_send
    scratch = [
        pltpu.VMEM((rows, channels), BF16),
        pltpu.VMEM((n, hidden, channels), BF16),
        pltpu.SemaphoreType.DMA((len(pieces),)),
        pltpu.SemaphoreType.DMA((4 * n - 3,)),
    ]
    if n_send:
        scratch.append(pltpu.SemaphoreType.DMA((n_send,)))
    extra = [before] if last else []
    return pl.pallas_call(
        functools.partial(proj0_kernel, pieces, rows, n, len(srcs), last),
        out_shape=outs,
        in_specs=[INV] * n + [HBM] + [ANY] * (len(sends) + len(srcs)) + [INV] * len(extra),
        out_specs=[INV] * 3 + [ANY] * n_send,
        scratch_shapes=scratch,
        compiler_params=PARAMS,
        name=f"proj0_{int(last)}",
    )(*inners, w_proj, *sends, *srcs, *extra)


def proj1_kernel(first, n, last, *rest):
    inners, w_hbm, sends, state = rest[:n], rest[n], rest[n + 1 : 3 * n - 1], rest[3 * n - 1]
    out, xbuf, obuf, wbuf, sems, wsems = rest[3 * n + int(last) :]
    rows, width = xbuf.shape
    cols = columns(0, n, width)
    copies = weight_copies(1, cols, w_hbm, halves(sends), wbuf, wsems)
    copies.append(copy(state.at[:, cols], xbuf, sems.at[0]))
    run(copies)
    for col in range(0, width, 128):
        cs = slice(col, col + 128)
        obuf[:, cs] = (xbuf[:, cs].astype(F32) + update_of(inners, wbuf, cs)).astype(BF16)
    run([copy(obuf, out.at[pl.ds(first, rows)], sems.at[1])])


def proj1(first, total, inners, w_proj, sends, state, before=None):
    hidden, channels = w_proj.shape[1:]
    n = len(inners)
    width = channels // n
    rows = state.shape[0]
    last = before is not None
    extra = [before] if last else []
    return pl.pallas_call(
        functools.partial(proj1_kernel, first, n, last),
        out_shape=shape((total, width), BF16),
        in_specs=[INV] * n + [HBM] + [ANY] * (len(sends) + 1) + [HBM] * len(extra),
        out_specs=HBM,
        scratch_shapes=[
            pltpu.VMEM((rows, width), BF16),
            pltpu.VMEM((rows, width), BF16),
            pltpu.VMEM((n, hidden, width), BF16),
            pltpu.SemaphoreType.DMA((2,)),
            pltpu.SemaphoreType.DMA((2 * n - 1,)),
        ],
        input_output_aliases={n + 1 + len(sends) + 1: 0} if last else {},
        compiler_params=PARAMS,
        name=f"proj1_{first}",
    )(*inners, w_proj, *sends, state, *extra)


def on_device(signal, lengths, dilations, w_conv, w_proj, gains, biases):
    own = signal[0]
    rows = own.shape[0]
    half = rows // 2
    cut, end = half + HALO, rows - HALO
    n_seq, n = lax.axis_size("seq"), lax.axis_size("chan")
    up = [(i, i + 1) for i in range(n_seq - 1)]
    down = [(i + 1, i) for i in range(n_seq - 1)]
    perm = lax.ppermute

    def ahead(value, k):
        return perm(value, "chan", [(i, (i + k) % n) for i in range(n)])

    def others(value):
        return [ahead(value, k) for k in range(1, n)]

    sums, edge, part_a, part_b, wsend = pre(own, w_proj, gains, biases, cut)
    stat, joined = join([sums] + others(sums))
    edges = others(edge)
    rest_a, rest_b = others(part_a), others(part_b)
    low, high = edge_rows(own, edges)
    low0, high0 = perm(low, "seq", up), perm(high, "seq", down)
    keep = keeps(lengths, dilations, rows)
    stats0 = batch_stats(stat, rows, joined, 0)

    sends0 = []
    for w in others(wsend):
        w2 = perm(w, "groups", SWAP)
        sends0 += [w, w2, perm(w, "dp", SWAP), perm(w2, "dp", SWAP)]

    srcs = (own, low0, high0, *edges, *rest_a, *rest_b)
    behind = [(k, 2 + k, 1 + n + k, 2 * n + k) for k in range(1, n)]
    pieces_a = [(1, 0, HALO, 0, None), (0, 0, cut, HALO, 0)]
    pieces_b = [(0, half - HALO, half + HALO, 0, 0), (2, 0, HALO, half + HALO, None)]
    res_a, res_b = [(0, 0, half, 0, 0)], [(0, half, half, 0, 0)]
    for k, e, a, b in behind:
        pieces_a += [(e, 0, HALO, HALO, k), (a, 0, cut - HALO, 2 * HALO, k)]
        pieces_b += [
            (a, half - 2 * HALO, 2 * HALO, 0, k),
            (b, 0, end - cut, 2 * HALO, k),
            (e, HALO, HALO, 2 * HALO + end - cut, k),
        ]
        res_a += [(e, 0, HALO, 0, k), (a, 0, half - HALO, HALO, k)]
        res_b += [
            (a, half - HALO, HALO, 0, k),
            (b, 0, end - cut, HALO, k),
            (e, HALO, HALO, HALO + end - cut, k),
        ]
    early = srcs[: 1 + 2 * n]
    inner_a = conv(pieces_a, early, n, 0, half, 0, dilations, stats0, keep, w_conv)
    inner_b = conv(pieces_b, srcs, n, 0, half, half, dilations, stats0, keep, w_conv)
    inners_a = [inner_a] + others(inner_a)
    inners_b = [inner_b] + others(inner_b)
    state_a, stat_a, edge_a, *wsend1 = proj0(res_a, early, half, inners_a, w_proj, sends0)
    state_b, stat, edge_b = proj0(res_b, srcs, half, inners_b, w_proj, sends0, stat_a)
    high1, low1 = perm(edge_a, "seq", down), perm(edge_b, "seq", up)
    stats1 = batch_stats(stat, rows, joined, 1)
    sends1 = []
    for k, w in enumerate(wsend1):
        w = ahead(w, k + 1)
        sends1 += [w, perm(w, "dp", SWAP)]

    srcs = (state_a, state_b, low1, high1)
    pieces_a = ((2, 0, HALO, 0, None), (0, 0, half, HALO, None), (1, 0, HALO, half + HALO, None))
    pieces_b = (
        (0, half - HALO, HALO, 0, None),
        (1, 0, half, HALO, None),
        (3, 0, HALO, half + HALO, None),
    )
    inner_a = conv(pieces_a, srcs, n, 1, half, 0, dilations, stats1, keep, w_conv)
    inner_b = conv(pieces_b, srcs, n, 1, half, half, dilations, stats1, keep, w_conv)
    inners_a = [inner_a] + others(inner_a)
    inners_b = [inner_b] + others(inner_b)
    out = proj1(0, rows, inners_a, w_proj, sends1, state_a)
    return proj1(half, rows, inners_b, w_proj, sends1, state_b, out)[None]


def solution(mesh):
    placed = (
        P(("groups", "dp"), "seq", "chan"),
        P(("groups", "dp"), None),
        P(),
        P(None, None, None, "chan"),
        P(None, "chan", None),
        P(None, "chan"),
        P(None, "chan"),
    )
    return jax.shard_map(
        on_device,
        mesh=mesh,
        in_specs=placed,
        out_specs=P(("groups", "dp"), "seq", "chan"),
        check_vma=False,
    )
```

```python
import functools

import jax
import jax.numpy as jnp
from jax import lax
from jax.experimental import pallas as pl
from jax.experimental.pallas import tpu as pltpu
from jax.sharding import PartitionSpec as P

HALO = 64
EPS = 1e-05
F32 = jnp.float32
BF16 = jnp.bfloat16
SWAP = [(0, 1), (1, 0)]

ANY = pl.BlockSpec(memory_space=pl.ANY)
HBM = pl.BlockSpec(memory_space=pltpu.HBM)
INV = pl.BlockSpec(memory_space=pltpu.VMEM)
INS = pl.BlockSpec(memory_space=pltpu.SMEM)
FREE = pl.CostEstimate(flops=0, transcendentals=0, bytes_accessed=0)


def limit(mib):
    return pltpu.CompilerParams(vmem_limit_bytes=mib << 20)


dot = functools.partial(jnp.dot, preferred_element_type=F32)
copy = pltpu.make_async_copy


def shape(dims, dtype):
    return jax.ShapeDtypeStruct(tuple(dims), dtype)


def gelu(x):
    return jax.nn.gelu(x)


def side_of(back, n):
    return lax.rem(lax.axis_index("chan") - back + n, n)


def columns(back, n, width):
    return pl.ds(pl.multiple_of(side_of(back, n) * width, 128), width)


def run(copies):
    for c in copies:
        c.start()
    for c in copies:
        c.wait()


def sums_about(v, pivot):
    gap = (v - pivot).reshape(v.shape[0] // 8, 8, v.shape[1])
    return jnp.sum(gap, axis=0), jnp.sum(gap * gap, axis=0)


def spread_of(pivot, s1, s2, rows):
    s1 = jnp.sum(s1, axis=0, keepdims=True)
    s2 = jnp.sum(s2, axis=0, keepdims=True)
    off = s1 * (1.0 / rows)
    return pivot + off, s2 - s1 * off


def merged(a, b, n):
    gap = a[0:1] - b[0:1]
    return (a[0:1] + b[0:1]) * 0.5, a[1:2] + b[1:2] + gap * gap * (0.5 * n)


def pre_kernel(x, out):
    rows = x.shape[0]
    pivot = jnp.mean(x[0:16, :].astype(F32)[0:8], axis=0, keepdims=True)
    s1 = s2 = jnp.zeros((8, x.shape[1]), F32)
    for r in range(0, rows, 64):
        t1, t2 = sums_about(x[r : r + 64, :].astype(F32), pivot)
        s1, s2 = s1 + t1, s2 + t2
    out[0:1, :], out[1:2, :] = spread_of(pivot, s1, s2, rows)


def pre(own):
    return pl.pallas_call(
        pre_kernel,
        out_shape=shape((2, own.shape[1]), F32),
        in_specs=[INV],
        out_specs=INV,
        compiler_params=limit(2),
        cost_estimate=FREE,
        name="pre",
    )(own)


def merge_kernel(n, a, b, out):
    out[0:1, :], out[1:2, :] = merged(a[...], b[...], n)


def scale_of(m2, n, gain):
    return lax.rsqrt(m2 * (1.0 / n) + EPS) * gain


def finish0_kernel(n, a, b, gains, biases, _, out):
    mean, m2 = merged(a[...], b[...], n)
    out[0:1, :] = mean
    out[1:2, :] = scale_of(m2, 2 * n, gains[0:1, :])
    out[2:3, :] = biases[0:1, :]
    out[3:4, :] = gains[1:2, :]
    out[4:5, :] = biases[1:2, :]


def finish1_kernel(n, a, b, joined, out):
    mean, m2 = merged(a[...], b[...], n)
    out[0:1, :] = mean
    out[1:2, :] = scale_of(m2, 2 * n, joined[3:4, :])
    out[2:3, :] = joined[4:5, :]


def batch_stats(stat, n, kernel, extra):
    steps = []
    for axis in ("dp", "seq"):
        size, step = lax.axis_size(axis), 1
        while step < size:
            steps.append((axis, [(i, i ^ step) for i in range(size)]))
            step *= 2
    channels = stat.shape[1]
    for at, (axis, pairs) in enumerate(steps):
        other = lax.ppermute(stat, axis, pairs)
        last = at == len(steps) - 1
        more = extra if last else ()
        stat = pl.pallas_call(
            functools.partial(kernel if last else merge_kernel, n),
            out_shape=shape((8 if last else 2, channels), F32),
            in_specs=[INV] * (2 + min(len(more), 2)) + [ANY] * max(len(more) - 2, 0),
            out_specs=INV,
            compiler_params=limit(1),
            cost_estimate=FREE,
            name="finish" if last else "merge",
        )(stat, other, *more)
        n *= 2
    return stat


def join_kernel(n, *refs):
    vecs, xs, w = refs[:n], refs[n : 2 * n], refs[2 * n]
    joined, low, high, wsend, lows, highs, sems, wsem = refs[2 * n + 1 :]
    rows = xs[0].shape[0]
    part = wsend.shape[0]
    quarter = lax.axis_index("groups") * 2 + lax.axis_index("dp")
    move = copy(w.at[0, pl.ds(pl.multiple_of(quarter * part, 16), part)], wsend, wsem)
    move.start()
    copies = []
    for k, x in enumerate(xs):
        copies.append(copy(x.at[pl.ds(rows - HALO, HALO)], lows.at[k], sems.at[2 * k]))
        copies.append(copy(x.at[pl.ds(0, HALO)], highs.at[k], sems.at[2 * k + 1]))
    for c in copies:
        c.start()
    for k, vec in enumerate(vecs):
        joined[:, columns(k, n, vec.shape[1])] = vec[...]
    for c in copies:
        c.wait()
    for k in range(n):
        cols = columns(k, n, xs[0].shape[1])
        low[:, cols] = lows[k]
        high[:, cols] = highs[k]
    move.wait()


def join(vecs, xs, w_proj):
    n, width = len(vecs), vecs[0].shape[1]
    part = w_proj.shape[1] // 4
    return pl.pallas_call(
        functools.partial(join_kernel, n),
        out_shape=(
            shape((8, n * width), F32),
            shape((HALO, n * width), BF16),
            shape((HALO, n * width), BF16),
            shape((part, w_proj.shape[2]), BF16),
        ),
        in_specs=[INV] * n + [ANY] * (n + 1),
        out_specs=(INV, INV, INV, ANY),
        scratch_shapes=[
            pltpu.VMEM((n, HALO, width), BF16),
            pltpu.VMEM((n, HALO, width), BF16),
            pltpu.SemaphoreType.DMA((2 * n,)),
            pltpu.SemaphoreType.DMA,
        ],
        compiler_params=limit(2),
        cost_estimate=FREE,
        name="join",
    )(*vecs, *xs, w_proj)


def keep_kernel(lengths, dilations, out):
    rows = out.shape[1]
    first = lax.axis_index("seq") * rows
    ends, end = [], jnp.int32(0)
    for k in range(lengths.shape[1]):
        end = end + lengths[0, k]
        ends.append(end)

    def segment(place):
        count = jnp.where(place >= 0, 1, 0)
        for end in ends:
            count = count + jnp.where(place >= end, 1, 0)
        return count

    @pl.loop(0, rows // 32)
    def _(i):
        at = pl.multiple_of(i * 32, 32)
        place = first + at + lax.broadcasted_iota(jnp.int32, (32, 128), 0)
        here = segment(place)
        for layer in range(2):
            d = dilations[layer]
            for side, there in enumerate((place - d, place + d)):
                keep = jnp.where(segment(there) == here, 1.0, 0.0)
                out[2 * layer + side, pl.ds(at, 32), :] = keep


def keeps(lengths, dilations, rows):
    return pl.pallas_call(
        keep_kernel,
        out_shape=shape((4, rows, 128), F32),
        in_specs=[INS, INS],
        out_specs=INV,
        compiler_params=limit(4),
                cost_estimate=FREE,
                name="keeps",
    )(lengths, dilations)


def shifted(ref, start, count):
    base = pl.multiple_of((start // 8) * 8, 8)
    tall = ref[pl.ds(base, count + 8), :]
    return pltpu.roll(tall, (count + 8 - (start - base)) % (count + 8), 0)[:count]


def piece(src, at, count, to, back, n, buf, sem):
    if back is None:
        dst = buf.at[pl.ds(to, count), :]
    else:
        dst = buf.at[pl.ds(to, count), columns(back, n, src.shape[1])]
    return copy(src.at[pl.ds(at, count), :], dst, sem)


def conv_kernel(pieces, layer, segs, ext, n, n_src, dilations, stats, keep, w_hbm, *rest):
    srcs, (out, xbuf, nbuf, wbuf, p0, p2, sems, wsems) = rest[:n_src], rest[n_src:]
    moves = [piece(srcs[p[0]], *p[1:], n, xbuf, sems.at[k]) for k, p in enumerate(pieces)]
    for m in moves:
        m.start()
    weights = [copy(w_hbm.at[layer, tap], wbuf.at[tap], wsems.at[tap]) for tap in range(3)]
    for w in weights:
        w.start()
    for m in moves:
        m.wait()
    block = 16
    mean, scale, bias = stats[0:1, :], stats[1:2, :], stats[2:3, :]

    @pl.loop(0, ext // block)
    def _(i):
        at = pl.ds(pl.multiple_of(i * block, block), block)
        v = xbuf[at, :].astype(F32)
        nbuf[at, :] = gelu((v - mean) * scale + bias).astype(BF16)

    weights[0].wait()
    p0[0 : ext - HALO, :] = dot(nbuf[0 : ext - HALO, :], wbuf[0])
    weights[2].wait()
    p2[0 : ext - HALO, :] = dot(nbuf[HALO:ext, :], wbuf[2])
    weights[1].wait()
    mid = dot(nbuf[HALO : ext - HALO, :], wbuf[1])
    d = dilations[layer]
    width = out.shape[1]
    to = 0
    for first, count in segs:
        base = to + 2 * HALO * segs.index((first, count))
        for r in range(0, count, HALO):
            left = shifted(p0, base + r + HALO - d, HALO)
            right = shifted(p2, base + r + d, HALO)
            here = slice(first + r, first + r + HALO)
            for c in range(0, width, 128):
                wide = min(128, width - c)
                cs = slice(c, c + wide)
                kl, kr = keep[2 * layer, here, :wide] > 0, keep[2 * layer + 1, here, :wide] > 0
                mixed = jnp.where(kl, left[:, cs], 0.0) + jnp.where(kr, right[:, cs], 0.0)
                mixed = mid[base + r : base + r + HALO, cs] + mixed
                out[to + r : to + r + HALO, cs] = gelu(mixed).astype(BF16)
        to += count


def conv(pieces, srcs, n, layer, segs, dilations, stats, keep, w_conv):
    channels, width = w_conv.shape[2:]
    rows = sum(count for _, count in segs)
    ext = rows + 2 * HALO * len(segs)
    return pl.pallas_call(
        functools.partial(conv_kernel, pieces, layer, segs, ext, n, len(srcs)),
        out_shape=shape((rows, width), BF16),
        in_specs=[INS, INV, INV, HBM] + [ANY] * len(srcs),
        out_specs=INV,
        scratch_shapes=[
            pltpu.VMEM((ext, channels), BF16),
            pltpu.VMEM((ext, channels), BF16),
            pltpu.VMEM((3, channels, width), BF16),
            pltpu.VMEM((ext - HALO + 8, width), F32),
            pltpu.VMEM((ext - HALO + 8, width), F32),
            pltpu.SemaphoreType.DMA((len(pieces),)),
            pltpu.SemaphoreType.DMA((3,)),
        ],
        compiler_params=limit(12),
        cost_estimate=FREE,
        name=f"conv{layer}_{len(segs)}",
    )(dilations, stats, keep, w_conv, *srcs)


def weight_copies(layer, cols, w_hbm, sends, wbuf, sems):
    copies = [copy(w_hbm.at[layer, :, cols], wbuf.at[0], sems.at[0])]
    for k, parts in enumerate(sends):
        size = parts[0][0].shape[0]
        for src, at in parts:
            dst = wbuf.at[k + 1, pl.ds(pl.multiple_of(at * size, 16), size), :]
            copies.append(copy(src, dst, sems.at[len(copies)]))
    return copies


def quarters(refs):
    group, core = lax.axis_index("groups"), lax.axis_index("dp")
    ats = (2 * group + core, 2 * (1 - group) + core, 2 * group + 1 - core, 3 - 2 * group - core)
    return [list(zip(refs[i : i + 4], ats)) for i in range(0, len(refs), 4)]


def halves(refs):
    core = lax.axis_index("dp")
    return [list(zip(refs[i : i + 2], (core, 1 - core))) for i in range(0, len(refs), 2)]


def update_of(inners, wbuf, cols):
    total = None
    for k, inner in enumerate(inners):
        term = dot(inner[...], wbuf[k, :, cols]).astype(BF16).astype(F32)
        total = term if total is None else total + term
    return total


def proj0_kernel(n, *rest):
    ins, edges, rest = rest[:n], rest[n : 2 * n], rest[2 * n :]
    w_hbm, sends, rest = rest[0], rest[1 : 4 * n - 3], rest[4 * n - 3 :]
    xs, (mid, low, high, stat, *wsend, xbuf, wbuf, sems, wsems, ssems) = rest[:n], rest[n:]
    rows = xbuf.shape[0]
    end = rows - HALO
    copies = weight_copies(0, slice(None), w_hbm, quarters(sends), wbuf, wsems)
    copies += [piece(x, 0, rows, 0, k, n, xbuf, sems.at[k]) for k, x in enumerate(xs)]
    moves = []
    for k, dst in enumerate(wsend):
        size, width = dst.shape
        ahead = lax.rem(lax.axis_index("chan") + k + 1, n) * width
        part = pl.ds(pl.multiple_of(lax.axis_index("dp") * size, 16), size)
        src = w_hbm.at[1, part, pl.ds(pl.multiple_of(ahead, 128), width)]
        moves.append(copy(src, dst, ssems.at[k]))
    for c in copies + moves:
        c.start()
    for c in copies:
        c.wait()
    for col in range(0, xbuf.shape[1], 256):
        cs = slice(col, col + 256)
        new = (xbuf[HALO:end, cs].astype(F32) + update_of(ins, wbuf, cs)).astype(BF16)
        mid[:, cs] = new
        v = new.astype(F32)
        pivot = jnp.mean(v[0:8], axis=0, keepdims=True)
        s1, s2 = sums_about(v, pivot)
        ends = update_of(edges, wbuf, cs)
        for dst, at, x in ((low, 0, 0), (high, HALO, end)):
            new = xbuf[x : x + HALO, cs].astype(F32) + ends[at : at + HALO]
            new = new.astype(BF16)
            dst[:, cs] = new
            t1, t2 = sums_about(new.astype(F32), pivot)
            s1, s2 = s1 + t1, s2 + t2
        stat[0:1, cs], stat[1:2, cs] = spread_of(pivot, s1, s2, rows)
    for m in moves:
        m.wait()


def proj0(inners, edges, w_proj, sends, xs):
    hidden, channels = w_proj.shape[1:]
    n = len(inners)
    rows = xs[0].shape[0]
    outs = [shape((rows - 2 * HALO, channels), BF16)]
    outs += [shape((HALO, channels), BF16)] * 2 + [shape((2, channels), F32)]
    outs += [shape((hidden // 2, channels // n), BF16)] * (n - 1)
    return pl.pallas_call(
        functools.partial(proj0_kernel, n),
        out_shape=outs,
        in_specs=[INV] * 2 * n + [HBM] + [ANY] * (len(sends) + n),
        out_specs=[INV] * 4 + [ANY] * (n - 1),
        scratch_shapes=[
            pltpu.VMEM((rows, channels), BF16),
            pltpu.VMEM((n, hidden, channels), BF16),
            pltpu.SemaphoreType.DMA((n,)),
            pltpu.SemaphoreType.DMA((4 * n - 3,)),
            pltpu.SemaphoreType.DMA((n - 1,)),
        ],
        compiler_params=limit(14),
        cost_estimate=FREE,
        name="proj0",
    )(*inners, *edges, w_proj, *sends, *xs)


def proj1_kernel(runs, n, n_src, last, *rest):
    inners, w_hbm, sends, rest = rest[:n], rest[n], rest[n + 1 : 3 * n - 1], rest[3 * n - 1 :]
    srcs, (out, xbuf, obuf, wbuf, sems, wsems) = rest[:n_src], rest[n_src + int(last) :]
    width = xbuf.shape[1]
    cols = columns(0, n, width)
    copies = weight_copies(1, cols, w_hbm, halves(sends), wbuf, wsems)
    at, outs = 0, []
    for k, (first, count) in enumerate(runs):
        here = pl.ds(at, count)
        copies.append(copy(srcs[k].at[:, cols], xbuf.at[here], sems.at[2 * k]))
        outs.append(copy(obuf.at[here], out.at[pl.ds(first, count)], sems.at[2 * k + 1]))
        at += count
    run(copies)
    for col in range(0, width, 128):
        cs = slice(col, col + 128)
        obuf[:, cs] = (xbuf[:, cs].astype(F32) + update_of(inners, wbuf, cs)).astype(BF16)
    run(outs)


def proj1(runs, total, inners, w_proj, sends, srcs, before=None):
    hidden, channels = w_proj.shape[1:]
    n = len(inners)
    width = channels // n
    rows = sum(count for _, count in runs)
    last = before is not None
    extra = [before] if last else []
    n_any = len(sends) + len(srcs)
    return pl.pallas_call(
        functools.partial(proj1_kernel, runs, n, len(srcs), last),
        out_shape=shape((total, width), BF16),
        in_specs=[INV] * n + [HBM] + [ANY] * n_any + [HBM] * len(extra),
        out_specs=HBM,
        scratch_shapes=[
            pltpu.VMEM((rows, width), BF16),
            pltpu.VMEM((rows, width), BF16),
            pltpu.VMEM((n, hidden, width), BF16),
            pltpu.SemaphoreType.DMA((2 * len(runs),)),
            pltpu.SemaphoreType.DMA((2 * n - 1,)),
        ],
        input_output_aliases={n + 1 + n_any: 0} if last else {},
        compiler_params=limit(6),
        cost_estimate=FREE,
        name=f"proj1_{rows}",
    )(*inners, w_proj, *sends, *srcs, *extra)


def on_device(signal, lengths, dilations, w_conv, w_proj, gains, biases):
    own = signal[0]
    rows = own.shape[0]
    end = rows - HALO
    n_seq, n = lax.axis_size("seq"), lax.axis_size("chan")
    up = [(i, i + 1) for i in range(n_seq - 1)]
    down = [(i + 1, i) for i in range(n_seq - 1)]
    perm = lax.ppermute

    def ahead(value, k):
        return perm(value, "chan", [(i, (i + k) % n) for i in range(n)])

    def others(value):
        return [ahead(value, k) for k in range(1, n)]

    w_conv = pltpu.with_memory_space_constraint(w_conv, pltpu.HBM)
    w_proj = pltpu.with_memory_space_constraint(w_proj, pltpu.HBM)
    xs = [own] + others(own)
    keep = keeps(lengths, dilations, rows)
    vec = batch_stats(pre(own), rows, finish0_kernel, (gains, biases, keep))
    joined, low, high, wsend = join([vec] + others(vec), xs, w_proj)
    low0, high0 = perm(low, "seq", up), perm(high, "seq", down)

    sent = others(wsend)

    inside, edges = ((HALO, end - HALO),), ((0, HALO), (end, HALO))
    pieces_a = [(k, 0, rows, 0, k) for k in range(n)]
    pieces_b = [(n, 0, HALO, 0, None), (n + 1, 0, HALO, 5 * HALO, None)]
    for k in range(n):
        pieces_b += [(k, 0, 2 * HALO, HALO, k), (k, end - HALO, 2 * HALO, 3 * HALO, k)]
    inner_a = conv(pieces_a, xs, n, 0, inside, dilations, joined, keep, w_conv)

    sent, inner_a = lax.optimization_barrier((sent, inner_a))
    swapped = [perm(w, "groups", SWAP) for w in sent]
    srcs = (*xs, low0, high0)
    inner_b = conv(pieces_b, srcs, n, 0, edges, dilations, joined, keep, w_conv)
    swapped, inner_b = lax.optimization_barrier((swapped, inner_b))
    sends0 = []
    for w, w2 in zip(sent, swapped):
        sends0 += [w, w2, perm(w, "dp", SWAP), perm(w2, "dp", SWAP)]
    inners_a = [inner_a] + others(inner_a)
    inners_b = [inner_b] + others(inner_b)
    mid, low, high, stat, *wsend1 = proj0(inners_a, inners_b, w_proj, sends0, xs)
    low1, high1 = perm(high, "seq", up), perm(low, "seq", down)
    stats1 = batch_stats(stat, rows, finish1_kernel, (joined,))
    sends1 = []
    for k, w in enumerate(wsend1):
        w = ahead(w, k + 1)
        sends1 += [w, perm(w, "dp", SWAP)]

    srcs = (low, mid, high, low1, high1)
    pieces_a = (
        (0, 0, HALO, 0, None),
        (1, 0, end - HALO, HALO, None),
        (2, 0, HALO, end, None),
    )
    pieces_b = (
        (3, 0, HALO, 0, None),
        (0, 0, HALO, HALO, None),
        (1, 0, HALO, 2 * HALO, None),
        (1, end - 2 * HALO, HALO, 3 * HALO, None),
        (2, 0, HALO, 4 * HALO, None),
        (4, 0, HALO, 5 * HALO, None),
    )
    inner_a = conv(pieces_a, srcs[:3], n, 1, inside, dilations, stats1, keep, w_conv)
    inner_b = conv(pieces_b, srcs, n, 1, edges, dilations, stats1, keep, w_conv)
    inners_a = [inner_a] + others(inner_a)
    inners_b = [inner_b] + others(inner_b)
    out = proj1(inside, rows, inners_a, w_proj, sends1, (mid,))
    return proj1(edges, rows, inners_b, w_proj, sends1, (low, high), out)[None]


def solution(mesh):
    placed = (
        P(("groups", "dp"), "seq", "chan"),
        P(("groups", "dp"), None),
        P(),
        P(None, None, None, "chan"),
        P(None, "chan", None),
        P(None, "chan"),
        P(None, "chan"),
    )
    return jax.shard_map(
        on_device,
        mesh=mesh,
        in_specs=placed,
        out_specs=P(("groups", "dp"), "seq", "chan"),
        check_vma=False,
    )
```

```python
import functools

import jax
import jax.numpy as jnp
from jax import lax
from jax.experimental import pallas as pl
from jax.experimental.pallas import tpu as pltpu
from jax.sharding import PartitionSpec as P

HALO = 64
EPS = 1e-05
F32 = jnp.float32
BF16 = jnp.bfloat16
SWAP = [(0, 1), (1, 0)]

ANY = pl.BlockSpec(memory_space=pl.ANY)
HBM = pl.BlockSpec(memory_space=pltpu.HBM)
INV = pl.BlockSpec(memory_space=pltpu.VMEM)
INS = pl.BlockSpec(memory_space=pltpu.SMEM)
FREE = pl.CostEstimate(flops=0, transcendentals=0, bytes_accessed=0)


def limit(mib):
    return pltpu.CompilerParams(vmem_limit_bytes=mib << 20)


dot = functools.partial(jnp.dot, preferred_element_type=F32)
copy = pltpu.make_async_copy


def shape(dims, dtype):
    return jax.ShapeDtypeStruct(tuple(dims), dtype)


def gelu(x):
    return jax.nn.gelu(x)


def side_of(back, n):
    return lax.rem(lax.axis_index("chan") - back + n, n)


def columns(back, n, width):
    return pl.ds(pl.multiple_of(side_of(back, n) * width, 128), width)


def run(copies):
    for c in copies:
        c.start()
    for c in copies:
        c.wait()


def sums_about(v, pivot):
    gap = (v - pivot).reshape(v.shape[0] // 8, 8, v.shape[1])
    return jnp.sum(gap, axis=0), jnp.sum(gap * gap, axis=0)


def spread_of(pivot, s1, s2, rows):
    s1 = jnp.sum(s1, axis=0, keepdims=True)
    s2 = jnp.sum(s2, axis=0, keepdims=True)
    off = s1 * (1.0 / rows)
    return pivot + off, s2 - s1 * off


def merged(a, b, n):
    gap = a[0:1] - b[0:1]
    return (a[0:1] + b[0:1]) * 0.5, a[1:2] + b[1:2] + gap * gap * (0.5 * n)


def pre_kernel(x, out):
    rows = x.shape[0]
    pivot = jnp.mean(x[0:16, :].astype(F32)[0:8], axis=0, keepdims=True)
    s1 = s2 = jnp.zeros((8, x.shape[1]), F32)
    for r in range(0, rows, 64):
        t1, t2 = sums_about(x[r : r + 64, :].astype(F32), pivot)
        s1, s2 = s1 + t1, s2 + t2
    out[0:1, :], out[1:2, :] = spread_of(pivot, s1, s2, rows)


def pre(own):
    return pl.pallas_call(
        pre_kernel,
        out_shape=shape((2, own.shape[1]), F32),
        in_specs=[INV],
        out_specs=INV,
        compiler_params=limit(2),
        cost_estimate=FREE,
        name="pre",
    )(own)


def merge_kernel(n, a, b, out):
    out[0:1, :], out[1:2, :] = merged(a[...], b[...], n)


def scale_of(m2, n, gain):
    return lax.rsqrt(m2 * (1.0 / n) + EPS) * gain


def finish0_kernel(n, a, b, gains, biases, _, out):
    mean, m2 = merged(a[...], b[...], n)
    out[0:1, :] = mean
    out[1:2, :] = scale_of(m2, 2 * n, gains[0:1, :])
    out[2:3, :] = biases[0:1, :]
    out[3:4, :] = gains[1:2, :]
    out[4:5, :] = biases[1:2, :]


def finish1_kernel(n, a, b, joined, *rest):
    out = rest[-1]
    mean, m2 = merged(a[...], b[...], n)
    out[0:1, :] = mean
    out[1:2, :] = scale_of(m2, 2 * n, joined[3:4, :])
    out[2:3, :] = joined[4:5, :]


def batch_stats(stat, n, kernel, extra, n_order):
    steps = []
    for axis in ("dp", "seq"):
        size, step = lax.axis_size(axis), 1
        while step < size:
            steps.append((axis, [(i, i ^ (2 * step - 1)) for i in range(size)]))
            step *= 2
    channels = stat.shape[1]
    found = []
    for at, (axis, pairs) in enumerate(steps):
        other = lax.ppermute(stat, axis, pairs)
        last = at == len(steps) - 1
        more = extra if last else ()
        stat = pl.pallas_call(
            functools.partial(kernel if last else merge_kernel, n),
            out_shape=shape((8 if last else 2, channels), F32),
            in_specs=[INV] * (2 + len(more) - (n_order if last else 0))
            + [ANY] * (n_order if last else 0),
            out_specs=INV,
            compiler_params=limit(1),
            cost_estimate=FREE,
            name="finish" if last else "merge",
        )(stat, other, *more)
        found.append(stat)
        n *= 2
    return found


def join_kernel(n, n_order, *refs):
    vecs, xs, w, refs = refs[:n], refs[n : 2 * n], refs[2 * n], refs[2 * n + 1 + n_order :]
    joined, send1, send2, wsend, *wsend1, sems = refs
    rows, width = xs[0].shape
    end = rows - HALO
    core, odd = lax.axis_index("dp"), lax.rem(lax.axis_index("seq"), 2)
    part = wsend.shape[0]
    quarter = lax.axis_index("groups") * 2 + core
    copies = [copy(w.at[0, pl.ds(pl.multiple_of(quarter * part, 16), part)], wsend, sems.at[0])]
    for k, dst in enumerate(wsend1):
        size = dst.shape[0]
        mine = pl.ds(pl.multiple_of(core * size, 16), size)
        src = w.at[1, mine, columns(-k - 1, n, width)]
        copies.append(copy(src, dst, sems.at[k + 1]))
    for c in copies:
        c.start()
    for k, (vec, x) in enumerate(zip(vecs, xs)):
        cols = columns(k, n, width)
        joined[:, cols] = vec[...]
        send1[:, cols] = x[pl.ds(pl.multiple_of((1 - odd) * end, HALO), HALO), :]
        send2[:, cols] = x[pl.ds(pl.multiple_of(odd * end, HALO), HALO), :]
    for c in copies:
        c.wait()


def join(vecs, xs, w_proj, order):
    n, width = len(vecs), vecs[0].shape[1]
    hidden, channels = w_proj.shape[1:]
    outs = [shape((8, channels), F32)] + [shape((HALO, channels), BF16)] * 2
    outs += [shape((hidden // 4, channels), BF16)]
    outs += [shape((hidden // 2, width), BF16)] * (n - 1)
    return pl.pallas_call(
        functools.partial(join_kernel, n, len(order)),
        out_shape=outs,
        in_specs=[INV] * (2 * n) + [ANY] * (1 + len(order)),
        out_specs=[INV] * 3 + [ANY] * n,
        scratch_shapes=[pltpu.SemaphoreType.DMA((n,))],
        compiler_params=limit(1),
        cost_estimate=FREE,
        name="join",
    )(*vecs, *xs, w_proj, *order)


def keep_kernel(lengths, dilations, out):
    rows = out.shape[1]
    first = lax.axis_index("seq") * rows
    ends, end = [], jnp.int32(0)
    for k in range(lengths.shape[1]):
        end = end + lengths[0, k]
        ends.append(end)

    def segment(place):
        count = jnp.where(place >= 0, 1, 0)
        for end in ends:
            count = count + jnp.where(place >= end, 1, 0)
        return count

    @pl.loop(0, rows // 32)
    def _(i):
        at = pl.multiple_of(i * 32, 32)
        place = first + at + lax.broadcasted_iota(jnp.int32, (32, 128), 0)
        here = segment(place)
        for layer in range(2):
            d = dilations[layer]
            for side, there in enumerate((place - d, place + d)):
                keep = jnp.where(segment(there) == here, 1.0, 0.0)
                out[2 * layer + side, pl.ds(at, 32), :] = keep


def keeps(lengths, dilations, rows):
    return pl.pallas_call(
        keep_kernel,
        out_shape=shape((4, rows, 128), F32),
        in_specs=[INS, INS],
        out_specs=INV,
        compiler_params=limit(4),
                cost_estimate=FREE,
                name="keeps",
    )(lengths, dilations)


def shifted(ref, start, count):
    base = pl.multiple_of((start // 8) * 8, 8)
    tall = ref[pl.ds(base, count + 8), :]
    return pltpu.roll(tall, (count + 8 - (start - base)) % (count + 8), 0)[:count]


def stage_kernel(w, *rest):
    layers, taps, _, width = w.shape
    outs, bufs, sems = rest[:layers], rest[layers:-1], rest[-1]
    step = outs[0].shape[1] // taps
    order = (0, 2, 1)
    copies = []
    for layer, out in enumerate(outs):
        for at, tap in enumerate(order):
            dst = bufs[0].at[layer, at] if bufs else out.at[:, pl.ds(at * step, width)]
            copies.append(copy(w.at[layer, tap], dst, sems.at[len(copies)]))
    run(copies)
    for buf in bufs:
        for layer, out in enumerate(outs):
            for at in range(taps):
                out[:, at * step : at * step + width] = buf[layer, at]


def stage(w_conv):
    layers, taps, channels, width = w_conv.shape
    step = -(-width // 128) * 128
    bufs = [] if step == width else [pltpu.VMEM(w_conv.shape, BF16)]
    return pl.pallas_call(
        stage_kernel,
        out_shape=[shape((channels, taps * step), BF16)] * layers,
        in_specs=[HBM],
        out_specs=[INV] * layers,
        scratch_shapes=bufs + [pltpu.SemaphoreType.DMA((layers * taps,))],
        compiler_params=limit(8 if bufs else 1),
        cost_estimate=FREE,
        name="stage",
    )(w_conv)


def conv_kernel(pieces, layer, segs, hand, n, n_src, n_order, dilations, stats, keep, w, *rest):
    srcs, (out, *kept, nbuf, p0, p2) = rest[:n_src], rest[n_src + n_order :]
    ext, width = nbuf.shape[0], out.shape[1]
    for src, at, count, to, back, raw in pieces:
        src = srcs[src]
        cols = slice(None) if back is None else columns(back, n, src.shape[1])
        if isinstance(to, tuple):
            odd = lax.rem(lax.axis_index("seq"), 2)
            to = pl.multiple_of(to[0] + odd * (to[1] - to[0]), HALO)
        if not raw:
            nbuf[to : to + count, cols] = src[at : at + count, :]
            continue
        mean, scale, bias = stats[0:1, cols], stats[1:2, cols], stats[2:3, cols]
        block = 128 if count % 128 == 0 else 64

        @pl.loop(0, count // block)
        def _(i):
            rows = pl.multiple_of(i * block, block)
            v = src[pl.ds(at + rows, block), :].astype(F32)
            dst = pl.ds(pl.multiple_of(to + rows, HALO), block)
            nbuf[dst, cols] = gelu((v - mean) * scale + bias).astype(BF16)

    step = w.shape[1] // 3
    sides = dot(nbuf[...], w[:, : 2 * step])
    p0[0 : ext - HALO, :] = sides[: ext - HALO, :width]
    p2[0 : ext - HALO, :] = sides[HALO:, step : step + width]
    mid = dot(nbuf[HALO : ext - HALO, :], w[:, 2 * step : 2 * step + width])
    d = dilations[layer]
    to = 0
    for k, (first, count) in enumerate(segs):
        base = to + 2 * HALO * k
        for r in range(0, count, HALO):
            left = shifted(p0, base + r + HALO - d, HALO)
            right = shifted(p2, base + r + d, HALO)
            here = slice(first + r, first + r + HALO)
            for c in range(0, width, 128):
                wide = min(128, width - c)
                cs = slice(c, c + wide)
                kl, kr = keep[2 * layer, here, :wide] > 0, keep[2 * layer + 1, here, :wide] > 0
                mixed = jnp.where(kl, left[:, cs], 0.0) + jnp.where(kr, right[:, cs], 0.0)
                mixed = mid[base + r : base + r + HALO, cs] + mixed
                out[to + r : to + r + HALO, cs] = gelu(mixed).astype(BF16)
        to += count
    for ref in kept:
        ref[...] = nbuf[hand : hand + 2 * HALO, :]


def conv(pieces, srcs, n, layer, segs, dilations, stats, keep, w, width, order, hand=None):
    channels = w.shape[0]
    rows = sum(count for _, count in segs)
    ext = rows + 2 * HALO * len(segs)
    outs = [shape((rows, width), BF16)]
    outs += [shape((2 * HALO, channels), BF16)] * int(hand is not None)
    cost = pl.CostEstimate(flops=0, transcendentals=0, bytes_accessed=24 << 20)
    return pl.pallas_call(
        functools.partial(conv_kernel, pieces, layer, segs, hand, n, len(srcs), len(order)),
        out_shape=outs,
        in_specs=[INS] + [INV] * (3 + len(srcs)) + [ANY] * len(order),
        out_specs=[INV] * len(outs),
        scratch_shapes=[
            pltpu.VMEM((ext, channels), BF16),
            pltpu.VMEM((ext - HALO + 8, width), F32),
            pltpu.VMEM((ext - HALO + 8, width), F32),
        ],
        compiler_params=limit(10),
        cost_estimate=cost,
        name=f"conv{layer}_{segs[0][0]}",
    )(dilations, stats, keep, w, *srcs, *order)


def weight_copies(sends, wbuf, sems):
    copies = []
    for k, parts in enumerate(sends):
        size = parts[0][0].shape[0]
        for src, at in parts:
            dst = wbuf.at[k, pl.ds(pl.multiple_of(at * size, 16), size), :]
            copies.append(copy(src, dst, sems.at[len(copies)]))
    return copies


def quarters(refs):
    group, core = lax.axis_index("groups"), lax.axis_index("dp")
    ats = (2 * group + core, 2 * (1 - group) + core, 2 * group + 1 - core, 3 - 2 * group - core)
    return [list(zip(refs[i : i + 4], ats)) for i in range(0, len(refs), 4)]


def halves(refs):
    core = lax.axis_index("dp")
    return [list(zip(refs[i : i + 2], (core, 1 - core))) for i in range(0, len(refs), 2)]


def update_of(inners, w, layer, cols, wbuf, others):
    total = dot(inners[0][...], w[layer, :, cols]).astype(BF16).astype(F32)
    for k, inner in enumerate(inners[1:]):
        total = total + dot(inner[...], wbuf[k, :, others]).astype(BF16).astype(F32)
    return total


def proj0_kernel(n, runs, *rest):
    chunks = [rest[i * n : (i + 1) * n] for i in range(len(runs))]
    rest = rest[len(runs) * n :]
    w, sends, rest = rest[0], rest[1 : 4 * n - 3], rest[4 * n - 3 :]
    xs, (mid, low, high, send1, send2, stat, wbuf, wsems) = rest[:n], rest[n:]
    rows, width = xs[0].shape
    end = rows - HALO
    run(weight_copies(quarters(sends), wbuf, wsems))
    even = lax.rem(lax.axis_index("seq"), 2) == 0
    for k, x in enumerate(xs):
        for col in range(0, width, 256):
            wide = min(256, width - col)
            here = slice(col, col + wide)
            cs = pl.ds(pl.multiple_of(side_of(k, n) * width + col, 128), wide)
            pivot, edge = None, {}
            for chunk, spans in zip(chunks, runs):
                update = update_of(chunk, w, 0, cs, wbuf, cs)
                at = 0
                for first, count in spans:
                    new = x[first : first + count, here].astype(F32) + update[at : at + count]
                    new = new.astype(BF16)
                    v = new.astype(F32)
                    if first in (0, end):
                        edge[first] = v
                        (high if first else low)[:, cs] = new
                    else:
                        mid[first - HALO : first - HALO + count, cs] = new
                    if pivot is None:
                        pivot = jnp.mean(v[0:8], axis=0, keepdims=True)
                        s1 = s2 = jnp.zeros((8, wide), F32)
                    t1, t2 = sums_about(v, pivot)
                    s1, s2 = s1 + t1, s2 + t2
                    at += count
            send1[:, cs] = jnp.where(even, edge[end], edge[0]).astype(BF16)
            send2[:, cs] = jnp.where(even, edge[0], edge[end]).astype(BF16)
            stat[0:1, cs], stat[1:2, cs] = spread_of(pivot, s1, s2, rows)


def proj0(runs, inners, w_proj, sends, xs):
    hidden, channels = w_proj.shape[1:]
    n = len(xs)
    rows = xs[0].shape[0]
    outs = [shape((rows - 2 * HALO, channels), BF16)]
    outs += [shape((HALO, channels), BF16)] * 4 + [shape((2, channels), F32)]
    return pl.pallas_call(
        functools.partial(proj0_kernel, n, runs),
        out_shape=outs,
        in_specs=[INV] * (len(runs) * n + 1) + [ANY] * len(sends) + [INV] * n,
        out_specs=[INV] * 6,
        scratch_shapes=[
            pltpu.VMEM((n - 1, hidden, channels), BF16),
            pltpu.SemaphoreType.DMA((4 * n - 4,)),
        ],
        compiler_params=limit(8),
        cost_estimate=FREE,
        name="proj0",
    )(*[x for chunk in inners for x in chunk], w_proj, *sends, *xs)


def proj1_kernel(runs, n, n_src, last, *rest):
    inners, w, sends, rest = rest[:n], rest[n], rest[n + 1 : 3 * n - 1], rest[3 * n - 1 :]
    srcs, (out, obuf, wbuf, sems, wsems) = rest[:n_src], rest[n_src + int(last) :]
    width = obuf.shape[1]
    run(weight_copies(halves(sends), wbuf, wsems))
    for col in range(0, width, 256):
        wide = min(256, width - col)
        here = slice(col, col + wide)
        cs = pl.ds(pl.multiple_of(side_of(0, n) * width + col, 128), wide)
        update = update_of(inners, w, 1, cs, wbuf, here)
        at = 0
        for (_, count, skip), src in zip(runs, srcs):
            new = src[skip : skip + count, cs].astype(F32) + update[at : at + count]
            obuf[at : at + count, here] = new.astype(BF16)
            at += count
    at, outs = 0, []
    for k, (first, count, _) in enumerate(runs):
        outs.append(copy(obuf.at[pl.ds(at, count)], out.at[pl.ds(first, count)], sems.at[k]))
        at += count
    run(outs)


def proj1(runs, total, inners, w_proj, sends, srcs, before=None):
    hidden, channels = w_proj.shape[1:]
    n = len(inners)
    width = channels // n
    rows = sum(count for _, count, _ in runs)
    last = before is not None
    extra = [before] if last else []
    return pl.pallas_call(
        functools.partial(proj1_kernel, runs, n, len(srcs), last),
        out_shape=shape((total, width), BF16),
        in_specs=[INV] * (n + 1)
        + [ANY] * len(sends)
        + [INV] * len(srcs)
        + [HBM] * len(extra),
        out_specs=HBM,
        scratch_shapes=[
            pltpu.VMEM((rows, width), BF16),
            pltpu.VMEM((n - 1, hidden, width), BF16),
            pltpu.SemaphoreType.DMA((len(runs),)),
            pltpu.SemaphoreType.DMA((2 * n - 2,)),
        ],
        input_output_aliases={n + 1 + len(sends) + len(srcs): 0} if last else {},
        compiler_params=limit(5),
        cost_estimate=FREE,
        name=f"proj1_{runs[0][0]}",
    )(*inners, w_proj, *sends, *srcs, *extra)


def on_device(signal, lengths, dilations, w_conv, w_proj, gains, biases):
    own = signal[0]
    rows = own.shape[0]
    width = w_conv.shape[3]
    end = rows - HALO
    n_seq, n = lax.axis_size("seq"), lax.axis_size("chan")
    pairs1 = [(i, i ^ 1) for i in range(n_seq)]
    pairs2 = [(i, i + 1 if i % 2 else i - 1) for i in range(1, n_seq - 1)]
    perm = lax.ppermute
    pinned = pltpu.with_memory_space_constraint
    tied = lax.optimization_barrier

    def others(value):
        return [perm(value, "chan", [(i, (i + k) % n) for i in range(n)]) for k in range(1, n)]

    sent = others(own)
    own = pinned(own, pltpu.VMEM)
    xs = [own] + [pinned(x, pltpu.VMEM) for x in sent]
    taps = [pinned(w, pltpu.VMEM) for w in stage(pinned(w_conv, pltpu.HBM))]
    keep = pinned(keeps(lengths, dilations, rows), pltpu.VMEM)
    found = batch_stats(pre(own), rows, finish0_kernel, (gains, biases, keep), 1)
    w_proj = pinned(w_proj, pltpu.VMEM)
    vecs = [found[-1]] + others(found[-1])
    joined, send1, send2, wsend, *wsend1 = join(vecs, xs, w_proj, taps)
    sent = others(wsend)

    half = rows // 2
    runs = (((HALO, half - HALO),), ((half, half - HALO),), ((0, HALO), (end, HALO)))
    at1, at2 = (5 * HALO, 0), (0, 5 * HALO)

    def inner_rows(layer, chunk, pieces, srcs, stats, *order):
        hand = chunk * (half - HALO)
        return conv(
            pieces,
            srcs,
            n,
            layer,
            runs[chunk],
            dilations,
            stats,
            keep,
            taps[layer],
            width,
            order,
            hand,
        )

    def edge_rows(layer, kept, halos, stats, *order):
        pieces = [(0, 0, 2 * HALO, HALO, None, False), (1, 0, 2 * HALO, 3 * HALO, None, False)]
        srcs = list(kept)
        for halo, at in zip(halos, (at1, at2)):
            pieces += [(len(srcs), 0, HALO, at, None, True)]
            srcs += [halo]
        return conv(
            pieces, srcs, n, layer, runs[2], dilations, stats, keep, taps[layer], width, order
        )[0]

    tall = half + HALO
    pieces_a = [(k, 0, tall, 0, k, True) for k in range(n)]
    pieces_b = [(k, half - HALO, tall, 0, k, True) for k in range(n)]
    inner_a, kept_a = inner_rows(0, 0, pieces_a, xs, joined)
    send1, send2, sent, inner_a = tied((send1, send2, sent, inner_a))
    halos = perm(send1, "seq", pairs1), perm(send2, "seq", pairs2)
    swapped = [perm(w, "groups", SWAP) for w in sent]
    others_a = others(inner_a)
    inner_b, kept_b = inner_rows(0, 1, pieces_b, xs, joined, kept_a)
    inner_c = edge_rows(0, (kept_a, kept_b), halos, joined, *others_a)
    sends0 = []
    for w, w2 in zip(sent, swapped):
        sends0 += [w, w2, perm(w, "dp", SWAP), perm(w2, "dp", SWAP)]
    inners = [[inner_a] + others_a] + [[inner] + others(inner) for inner in (inner_b, inner_c)]
    mid, low, high, send1, send2, stat = proj0(runs, inners, w_proj, sends0, xs)
    found = batch_stats(stat, rows, finish1_kernel, (joined,), 0)
    stats1 = found[-1]
    wsend1, _ = tied((wsend1, found[0]))
    sends1 = []
    for k, w in enumerate(wsend1):
        w = perm(w, "chan", [(i, (i + k + 1) % n) for i in range(n)])
        sends1 += [w, perm(w, "dp", SWAP)]
    send1, send2, _ = tied((send1, send2, stats1))
    halos = perm(send1, "seq", pairs1), perm(send2, "seq", pairs2)

    pieces_a = ((0, 0, HALO, 0, None, True), (1, 0, half, HALO, None, True))
    pieces_b = (
        (1, half - 2 * HALO, half, 0, None, True),
        (2, 0, HALO, half, None, True),
    )
    inner_a, kept_a = inner_rows(1, 0, pieces_a, (low, mid), stats1)
    inner_b, kept_b = inner_rows(1, 1, pieces_b, (low, mid, high), stats1, kept_a)
    inner_c = edge_rows(1, (kept_a, kept_b), halos, stats1)
    inners = [[inner] + others(inner) for inner in (inner_a, inner_b, inner_c)]
    out = proj1(((HALO, half - HALO, 0),), rows, inners[0], w_proj, sends1, (mid,))
    out = proj1(((half, half - HALO, half - HALO),), rows, inners[1], w_proj, sends1, (mid,), out)
    ends = ((0, HALO, 0), (end, HALO, 0))
    return proj1(ends, rows, inners[2], w_proj, sends1, (low, high), out)[None]


def solution(mesh):
    placed = (
        P(("groups", "dp"), "seq", "chan"),
        P(("groups", "dp"), None),
        P(),
        P(None, None, None, "chan"),
        P(None, "chan", None),
        P(None, "chan"),
        P(None, "chan"),
    )
    return jax.shard_map(
        on_device,
        mesh=mesh,
        in_specs=placed,
        out_specs=P(("groups", "dp"), "seq", "chan"),
        check_vma=False,
    )
```

```python
import functools

import jax
import jax.numpy as jnp
from jax import lax
from jax.experimental import pallas as pl
from jax.experimental.pallas import tpu as pltpu
from jax.sharding import PartitionSpec as P

HALO = 64
EPS = 1e-05
F32 = jnp.float32
BF16 = jnp.bfloat16
SWAP = [(0, 1), (1, 0)]

ANY = pl.BlockSpec(memory_space=pl.ANY)
HBM = pl.BlockSpec(memory_space=pltpu.HBM)
INV = pl.BlockSpec(memory_space=pltpu.VMEM)
INS = pl.BlockSpec(memory_space=pltpu.SMEM)
FREE = pl.CostEstimate(flops=0, transcendentals=0, bytes_accessed=0)


def limit(mib):
    return pltpu.CompilerParams(vmem_limit_bytes=mib << 20)


dot = functools.partial(jnp.dot, preferred_element_type=F32)
copy = pltpu.make_async_copy


def shape(dims, dtype):
    return jax.ShapeDtypeStruct(tuple(dims), dtype)


def gelu(x):
    return jax.nn.gelu(x)


def side_of(back, n):
    return lax.rem(lax.axis_index("chan") - back + n, n)


def columns(back, n, width):
    return pl.ds(pl.multiple_of(side_of(back, n) * width, 128), width)


def run(copies):
    for c in copies:
        c.start()
    for c in copies:
        c.wait()


def sums_about(v, pivot):
    gap = (v - pivot).reshape(v.shape[0] // 8, 8, v.shape[1])
    return jnp.sum(gap, axis=0), jnp.sum(gap * gap, axis=0)


def spread_of(pivot, s1, s2, rows):
    s1 = jnp.sum(s1, axis=0, keepdims=True)
    s2 = jnp.sum(s2, axis=0, keepdims=True)
    off = s1 * (1.0 / rows)
    return pivot + off, s2 - s1 * off


def merged(a, b, n):
    gap = a[0:1] - b[0:1]
    return (a[0:1] + b[0:1]) * 0.5, a[1:2] + b[1:2] + gap * gap * (0.5 * n)


def pre_kernel(x, out):
    rows = x.shape[0]
    pivot = jnp.mean(x[0:16, :].astype(F32)[0:8], axis=0, keepdims=True)
    s1 = s2 = jnp.zeros((8, x.shape[1]), F32)
    for r in range(0, rows, 64):
        t1, t2 = sums_about(x[r : r + 64, :].astype(F32), pivot)
        s1, s2 = s1 + t1, s2 + t2
    out[0:1, :], out[1:2, :] = spread_of(pivot, s1, s2, rows)


def pre(own):
    return pl.pallas_call(
        pre_kernel,
        out_shape=shape((2, own.shape[1]), F32),
        in_specs=[INV],
        out_specs=INV,
        compiler_params=limit(2),
        cost_estimate=FREE,
        name="pre",
    )(own)


def merge_kernel(n, a, b, out):
    out[0:1, :], out[1:2, :] = merged(a[...], b[...], n)


def scale_of(m2, n, gain):
    return lax.rsqrt(m2 * (1.0 / n) + EPS) * gain


def finish0_kernel(n, a, b, gains, biases, _, out):
    mean, m2 = merged(a[...], b[...], n)
    out[0:1, :] = mean
    out[1:2, :] = scale_of(m2, 2 * n, gains[0:1, :])
    out[2:3, :] = biases[0:1, :]
    out[3:4, :] = gains[1:2, :]
    out[4:5, :] = biases[1:2, :]


def finish1_kernel(n, a, b, joined, *rest):
    out = rest[-1]
    mean, m2 = merged(a[...], b[...], n)
    out[0:1, :] = mean
    out[1:2, :] = scale_of(m2, 2 * n, joined[3:4, :])
    out[2:3, :] = joined[4:5, :]


def batch_stats(stat, n, kernel, extra, n_order):
    steps = []
    for axis in ("dp", "seq"):
        size, step = lax.axis_size(axis), 1
        while step < size:
            steps.append((axis, [(i, i ^ (2 * step - 1)) for i in range(size)]))
            step *= 2
    channels = stat.shape[1]
    found = []
    for at, (axis, pairs) in enumerate(steps):
        other = lax.ppermute(stat, axis, pairs)
        last = at == len(steps) - 1
        more = extra if last else ()
        stat = pl.pallas_call(
            functools.partial(kernel if last else merge_kernel, n),
            out_shape=shape((8 if last else 2, channels), F32),
            in_specs=[INV] * (2 + len(more) - (n_order if last else 0))
            + [ANY] * (n_order if last else 0),
            out_specs=INV,
            compiler_params=limit(1),
            cost_estimate=FREE,
            name="finish" if last else "merge",
        )(stat, other, *more)
        found.append(stat)
        n *= 2
    return found


def join_kernel(n, n_order, *refs):
    vecs, xs, (joined, send1, send2) = refs[:n], refs[n : 2 * n], refs[2 * n + n_order :]
    rows, width = xs[0].shape
    end = rows - HALO
    odd = lax.rem(lax.axis_index("seq"), 2)
    for k, (vec, x) in enumerate(zip(vecs, xs)):
        cols = columns(k, n, width)
        joined[:, cols] = vec[...]
        send1[:, cols] = x[pl.ds(pl.multiple_of((1 - odd) * end, HALO), HALO), :]
        send2[:, cols] = x[pl.ds(pl.multiple_of(odd * end, HALO), HALO), :]


def join(vecs, xs, order):
    n, width = len(vecs), vecs[0].shape[1]
    outs = [shape((8, n * width), F32)] + [shape((HALO, n * width), BF16)] * 2
    return pl.pallas_call(
        functools.partial(join_kernel, n, len(order)),
        out_shape=outs,
        in_specs=[INV] * (2 * n) + [ANY] * len(order),
        out_specs=[INV] * 3,
        compiler_params=limit(1),
        cost_estimate=FREE,
        name="join",
    )(*vecs, *xs, *order)


def cut_kernel(n, w, _, wsend, *rest):
    wsend1, sems = rest[:-1], rest[-1]
    core = lax.axis_index("dp")
    part = wsend.shape[0]
    quarter = lax.axis_index("groups") * 2 + core
    copies = [copy(w.at[0, pl.ds(pl.multiple_of(quarter * part, 16), part)], wsend, sems.at[0])]
    for k, dst in enumerate(wsend1):
        size, width = dst.shape
        mine = pl.ds(pl.multiple_of(core * size, 16), size)
        src = w.at[1, mine, columns(-k - 1, n, width)]
        copies.append(copy(src, dst, sems.at[k + 1]))
    run(copies)


def cut(w_proj, n, order):
    hidden, channels = w_proj.shape[1:]
    outs = [shape((hidden // 4, channels), BF16)]
    outs += [shape((hidden // 2, channels // n), BF16)] * (n - 1)
    return pl.pallas_call(
        functools.partial(cut_kernel, n),
        out_shape=outs,
        in_specs=[ANY, ANY],
        out_specs=[ANY] * n,
        scratch_shapes=[pltpu.SemaphoreType.DMA((n,))],
        compiler_params=limit(1),
        cost_estimate=FREE,
        name="cut",
    )(w_proj, order)


def keep_kernel(lengths, dilations, out):
    rows = out.shape[1]
    first = lax.axis_index("seq") * rows
    ends, end = [], jnp.int32(0)
    for k in range(lengths.shape[1]):
        end = end + lengths[0, k]
        ends.append(end)

    def segment(place):
        count = jnp.where(place >= 0, 1, 0)
        for end in ends:
            count = count + jnp.where(place >= end, 1, 0)
        return count

    @pl.loop(0, rows // 32)
    def _(i):
        at = pl.multiple_of(i * 32, 32)
        place = first + at + lax.broadcasted_iota(jnp.int32, (32, 128), 0)
        here = segment(place)
        for layer in range(2):
            d = dilations[layer]
            for side, there in enumerate((place - d, place + d)):
                keep = jnp.where(segment(there) == here, 1.0, 0.0)
                out[2 * layer + side, pl.ds(at, 32), :] = keep


def keeps(lengths, dilations, rows):
    return pl.pallas_call(
        keep_kernel,
        out_shape=shape((4, rows, 128), F32),
        in_specs=[INS, INS],
        out_specs=INV,
        compiler_params=limit(4),
                cost_estimate=FREE,
                name="keeps",
    )(lengths, dilations)


def shifted(ref, start, count):
    base = pl.multiple_of((start // 8) * 8, 8)
    tall = ref[pl.ds(base, count + 8), :]
    return pltpu.roll(tall, (count + 8 - (start - base)) % (count + 8), 0)[:count]


def stage_kernel(w, *rest):
    layers, taps, _, width = w.shape
    outs, bufs, sems = rest[:layers], rest[layers:-1], rest[-1]
    step = outs[0].shape[1] // taps
    order = (0, 2, 1)
    copies = []
    for layer, out in enumerate(outs):
        for at, tap in enumerate(order):
            dst = bufs[0].at[layer, at] if bufs else out.at[:, pl.ds(at * step, width)]
            copies.append(copy(w.at[layer, tap], dst, sems.at[len(copies)]))
    run(copies)
    for buf in bufs:
        for layer, out in enumerate(outs):
            for at in range(taps):
                out[:, at * step : at * step + width] = buf[layer, at]


def stage(w_conv):
    layers, taps, channels, width = w_conv.shape
    step = -(-width // 128) * 128
    bufs = [] if step == width else [pltpu.VMEM(w_conv.shape, BF16)]
    return pl.pallas_call(
        stage_kernel,
        out_shape=[shape((channels, taps * step), BF16)] * layers,
        in_specs=[HBM],
        out_specs=[INV] * layers,
        scratch_shapes=bufs + [pltpu.SemaphoreType.DMA((layers * taps,))],
        compiler_params=limit(8 if bufs else 1),
        cost_estimate=FREE,
        name="stage",
    )(w_conv)


def conv_kernel(pieces, layer, segs, hand, n, n_src, n_order, dilations, stats, keep, w, *rest):
    srcs, (out, *kept, nbuf, p0, p2) = rest[:n_src], rest[n_src + n_order :]
    ext, width = nbuf.shape[0], out.shape[1]
    for src, at, count, to, back, raw in pieces:
        src = srcs[src]
        cols = slice(None) if back is None else columns(back, n, src.shape[1])
        if isinstance(to, tuple):
            odd = lax.rem(lax.axis_index("seq"), 2)
            to = pl.multiple_of(to[0] + odd * (to[1] - to[0]), HALO)
        if not raw:
            nbuf[to : to + count, cols] = src[at : at + count, :]
            continue
        mean, scale, bias = stats[0:1, cols], stats[1:2, cols], stats[2:3, cols]
        block = 128 if count % 128 == 0 else 64

        for rows in range(0, count, block):
            v = src[at + rows : at + rows + block, :].astype(F32)
            dst = pl.ds(pl.multiple_of(to + rows, HALO), block)
            nbuf[dst, cols] = gelu((v - mean) * scale + bias).astype(BF16)

    step = w.shape[1] // 3
    sides = dot(nbuf[...], w[:, : 2 * step])
    p0[0 : ext - HALO, :] = sides[: ext - HALO, :width]
    p2[0 : ext - HALO, :] = sides[HALO:, step : step + width]
    mid = dot(nbuf[HALO : ext - HALO, :], w[:, 2 * step : 2 * step + width])
    d = dilations[layer]
    to = 0
    for k, (first, count) in enumerate(segs):
        base = to + 2 * HALO * k
        for r in range(0, count, HALO):
            left = shifted(p0, base + r + HALO - d, HALO)
            right = shifted(p2, base + r + d, HALO)
            here = slice(first + r, first + r + HALO)
            for c in range(0, width, 128):
                wide = min(128, width - c)
                cs = slice(c, c + wide)
                kl, kr = keep[2 * layer, here, :wide] > 0, keep[2 * layer + 1, here, :wide] > 0
                mixed = jnp.where(kl, left[:, cs], 0.0) + jnp.where(kr, right[:, cs], 0.0)
                mixed = mid[base + r : base + r + HALO, cs] + mixed
                out[to + r : to + r + HALO, cs] = gelu(mixed).astype(BF16)
        to += count
    for ref in kept:
        ref[...] = nbuf[hand : hand + 2 * HALO, :]


def conv(pieces, srcs, n, layer, segs, dilations, stats, keep, w, width, order, hand=None):
    channels = w.shape[0]
    rows = sum(count for _, count in segs)
    ext = rows + 2 * HALO * len(segs)
    outs = [shape((rows, width), BF16)]
    outs += [shape((2 * HALO, channels), BF16)] * int(hand is not None)
    cost = pl.CostEstimate(flops=0, transcendentals=0, bytes_accessed=24 << 20)
    return pl.pallas_call(
        functools.partial(conv_kernel, pieces, layer, segs, hand, n, len(srcs), len(order)),
        out_shape=outs,
        in_specs=[INS] + [INV] * (3 + len(srcs)) + [ANY] * len(order),
        out_specs=[INV] * len(outs),
        scratch_shapes=[
            pltpu.VMEM((ext, channels), BF16),
            pltpu.VMEM((ext - HALO + 8, width), F32),
            pltpu.VMEM((ext - HALO + 8, width), F32),
        ],
        compiler_params=limit(10),
        cost_estimate=cost,
        name=f"conv{layer}_{segs[0][0]}",
    )(dilations, stats, keep, w, *srcs, *order)


def weight_copies(sends, wbuf, sems):
    copies = []
    for k, parts in enumerate(sends):
        size = parts[0][0].shape[0]
        for src, at in parts:
            dst = wbuf.at[k, pl.ds(pl.multiple_of(at * size, 16), size), :]
            copies.append(copy(src, dst, sems.at[len(copies)]))
    return copies


def quarters(refs):
    group, core = lax.axis_index("groups"), lax.axis_index("dp")
    ats = (2 * group + core, 2 * (1 - group) + core, 2 * group + 1 - core, 3 - 2 * group - core)
    return [list(zip(refs[i : i + 4], ats)) for i in range(0, len(refs), 4)]


def halves(refs):
    core = lax.axis_index("dp")
    return [list(zip(refs[i : i + 2], (core, 1 - core))) for i in range(0, len(refs), 2)]


def update_of(inners, w, layer, cols, wbuf, others):
    total = dot(inners[0][...], w[layer, :, cols]).astype(BF16).astype(F32)
    for k, inner in enumerate(inners[1:]):
        total = total + dot(inner[...], wbuf[k, :, others]).astype(BF16).astype(F32)
    return total


def proj0_kernel(n, runs, *rest):
    chunks = [rest[i * n : (i + 1) * n] for i in range(len(runs))]
    rest = rest[len(runs) * n :]
    w, sends, rest = rest[0], rest[1 : 4 * n - 3], rest[4 * n - 3 :]
    xs, (mid, low, high, send1, send2, stat, wbuf, wsems) = rest[:n], rest[n:]
    rows, width = xs[0].shape
    end = rows - HALO
    run(weight_copies(quarters(sends), wbuf, wsems))
    even = lax.rem(lax.axis_index("seq"), 2) == 0
    for k, x in enumerate(xs):
        for col in range(0, width, 256):
            wide = min(256, width - col)
            here = slice(col, col + wide)
            cs = pl.ds(pl.multiple_of(side_of(k, n) * width + col, 128), wide)
            pivot, edge = None, {}
            for chunk, spans in zip(chunks, runs):
                update = update_of(chunk, w, 0, cs, wbuf, cs)
                at = 0
                for first, count in spans:
                    new = x[first : first + count, here].astype(F32) + update[at : at + count]
                    new = new.astype(BF16)
                    v = new.astype(F32)
                    if first in (0, end):
                        edge[first] = v
                        (high if first else low)[:, cs] = new
                    else:
                        mid[first - HALO : first - HALO + count, cs] = new
                    if pivot is None:
                        pivot = jnp.mean(v[0:8], axis=0, keepdims=True)
                        s1 = s2 = jnp.zeros((8, wide), F32)
                    t1, t2 = sums_about(v, pivot)
                    s1, s2 = s1 + t1, s2 + t2
                    at += count
            send1[:, cs] = jnp.where(even, edge[end], edge[0]).astype(BF16)
            send2[:, cs] = jnp.where(even, edge[0], edge[end]).astype(BF16)
            stat[0:1, cs], stat[1:2, cs] = spread_of(pivot, s1, s2, rows)


def proj0(runs, inners, w_proj, sends, xs):
    hidden, channels = w_proj.shape[1:]
    n = len(xs)
    rows = xs[0].shape[0]
    outs = [shape((rows - 2 * HALO, channels), BF16)]
    outs += [shape((HALO, channels), BF16)] * 4 + [shape((2, channels), F32)]
    return pl.pallas_call(
        functools.partial(proj0_kernel, n, runs),
        out_shape=outs,
        in_specs=[INV] * (len(runs) * n + 1) + [ANY] * len(sends) + [INV] * n,
        out_specs=[INV] * 6,
        scratch_shapes=[
            pltpu.VMEM((n - 1, hidden, channels), BF16),
            pltpu.SemaphoreType.DMA((4 * n - 4,)),
        ],
        compiler_params=limit(8),
        cost_estimate=FREE,
        name="proj0",
    )(*[x for chunk in inners for x in chunk], w_proj, *sends, *xs)


def proj1_kernel(runs, n, n_src, last, *rest):
    inners, w, sends, rest = rest[:n], rest[n], rest[n + 1 : 3 * n - 1], rest[3 * n - 1 :]
    srcs, (out, obuf, wbuf, sems, wsems) = rest[:n_src], rest[n_src + int(last) :]
    width = obuf.shape[1]
    run(weight_copies(halves(sends), wbuf, wsems))
    for col in range(0, width, 256):
        wide = min(256, width - col)
        here = slice(col, col + wide)
        cs = pl.ds(pl.multiple_of(side_of(0, n) * width + col, 128), wide)
        update = update_of(inners, w, 1, cs, wbuf, here)
        at = 0
        for (_, count, skip), src in zip(runs, srcs):
            new = src[skip : skip + count, cs].astype(F32) + update[at : at + count]
            obuf[at : at + count, here] = new.astype(BF16)
            at += count
    at, outs = 0, []
    for k, (first, count, _) in enumerate(runs):
        outs.append(copy(obuf.at[pl.ds(at, count)], out.at[pl.ds(first, count)], sems.at[k]))
        at += count
    run(outs)


def proj1(runs, total, inners, w_proj, sends, srcs, before=None):
    hidden, channels = w_proj.shape[1:]
    n = len(inners)
    width = channels // n
    rows = sum(count for _, count, _ in runs)
    last = before is not None
    extra = [before] if last else []
    return pl.pallas_call(
        functools.partial(proj1_kernel, runs, n, len(srcs), last),
        out_shape=shape((total, width), BF16),
        in_specs=[INV] * (n + 1)
        + [ANY] * len(sends)
        + [INV] * len(srcs)
        + [HBM] * len(extra),
        out_specs=HBM,
        scratch_shapes=[
            pltpu.VMEM((rows, width), BF16),
            pltpu.VMEM((n - 1, hidden, width), BF16),
            pltpu.SemaphoreType.DMA((len(runs),)),
            pltpu.SemaphoreType.DMA((2 * n - 2,)),
        ],
        input_output_aliases={n + 1 + len(sends) + len(srcs): 0} if last else {},
        compiler_params=limit(5),
        cost_estimate=FREE,
        name=f"proj1_{runs[0][0]}",
    )(*inners, w_proj, *sends, *srcs, *extra)


def on_device(signal, lengths, dilations, w_conv, w_proj, gains, biases):
    own = signal[0]
    rows = own.shape[0]
    width = w_conv.shape[3]
    end = rows - HALO
    n_seq, n = lax.axis_size("seq"), lax.axis_size("chan")
    pairs1 = [(i, i ^ 1) for i in range(n_seq)]
    pairs2 = [(i, i + 1 if i % 2 else i - 1) for i in range(1, n_seq - 1)]
    perm = lax.ppermute
    pinned = pltpu.with_memory_space_constraint
    tied = lax.optimization_barrier

    def others(value):
        return [perm(value, "chan", [(i, (i + k) % n) for i in range(n)]) for k in range(1, n)]

    sent = others(own)
    own = pinned(own, pltpu.VMEM)
    xs = [own] + [pinned(x, pltpu.VMEM) for x in sent]
    taps = [pinned(w, pltpu.VMEM) for w in stage(pinned(w_conv, pltpu.HBM))]
    keep = pinned(keeps(lengths, dilations, rows), pltpu.VMEM)
    found = batch_stats(pre(own), rows, finish0_kernel, (gains, biases, keep), 1)
    w_proj = pinned(w_proj, pltpu.VMEM)
    vecs = [found[-1]]
    for k in range(1, n):
        pairs = []
        for z in range(n_seq):
            for c in range(n):
                pairs.append((z * n + c, (z ^ 1) * n + (c + k) % n))
        vecs.append(perm(found[-1], ("seq", "chan"), pairs))
    wsend, *wsend1 = cut(w_proj, n, found[-1])
    sent = others(wsend)
    joined, send1, send2 = join(vecs, xs, taps)

    half = rows // 2
    runs = (((HALO, half - HALO),), ((half, half - HALO),), ((0, HALO), (end, HALO)))
    at1, at2 = (5 * HALO, 0), (0, 5 * HALO)

    def inner_rows(layer, chunk, pieces, srcs, stats, *order):
        hand = chunk * (half - HALO)
        return conv(
            pieces,
            srcs,
            n,
            layer,
            runs[chunk],
            dilations,
            stats,
            keep,
            taps[layer],
            width,
            order,
            hand,
        )

    def edge_rows(layer, kept, halos, stats, *order):
        pieces = [(0, 0, 2 * HALO, HALO, None, False), (1, 0, 2 * HALO, 3 * HALO, None, False)]
        srcs = list(kept)
        for halo, at in zip(halos, (at1, at2)):
            pieces += [(len(srcs), 0, HALO, at, None, True)]
            srcs += [halo]
        return conv(
            pieces, srcs, n, layer, runs[2], dilations, stats, keep, taps[layer], width, order
        )[0]

    tall = half + HALO
    pieces_a = [(k, 0, tall, 0, k, True) for k in range(n)]
    pieces_b = [(k, half - HALO, tall, 0, k, True) for k in range(n)]
    inner_a, kept_a = inner_rows(0, 0, pieces_a, xs, joined)
    send1, send2, sent, inner_a = tied((send1, send2, sent, inner_a))
    halos = perm(send1, "seq", pairs1), perm(send2, "seq", pairs2)
    swapped = [perm(w, "groups", SWAP) for w in sent]
    others_a = others(inner_a)
    inner_b, kept_b = inner_rows(0, 1, pieces_b, xs, joined, kept_a)
    swapped, inner_b = tied((swapped, inner_b))
    inner_c = edge_rows(0, (kept_a, kept_b), halos, joined, *others_a)
    sends0 = []
    for w, w2 in zip(sent, swapped):
        sends0 += [w, w2, perm(w, "dp", SWAP), perm(w2, "dp", SWAP)]
    inners = [[inner_a] + others_a] + [[inner] + others(inner) for inner in (inner_b, inner_c)]
    mid, low, high, send1, send2, stat = proj0(runs, inners, w_proj, sends0, xs)
    found = batch_stats(stat, rows, finish1_kernel, (joined,), 0)
    stats1 = found[-1]
    wsend1, _ = tied((wsend1, found[0]))
    sends1 = []
    for k, w in enumerate(wsend1):
        w = perm(w, "chan", [(i, (i + k + 1) % n) for i in range(n)])
        sends1 += [w, perm(w, "dp", SWAP)]
    send1, send2, _ = tied((send1, send2, stats1))
    halos = perm(send1, "seq", pairs1), perm(send2, "seq", pairs2)

    pieces_a = ((0, 0, HALO, 0, None, True), (1, 0, half, HALO, None, True))
    pieces_b = (
        (1, half - 2 * HALO, half, 0, None, True),
        (2, 0, HALO, half, None, True),
    )
    inner_a, kept_a = inner_rows(1, 0, pieces_a, (low, mid), stats1)
    inner_b, kept_b = inner_rows(1, 1, pieces_b, (low, mid, high), stats1, kept_a)
    inner_c = edge_rows(1, (kept_a, kept_b), halos, stats1)
    inners = [[inner] + others(inner) for inner in (inner_a, inner_b, inner_c)]
    out = proj1(((HALO, half - HALO, 0),), rows, inners[0], w_proj, sends1, (mid,))
    out = proj1(((half, half - HALO, half - HALO),), rows, inners[1], w_proj, sends1, (mid,), out)
    ends = ((0, HALO, 0), (end, HALO, 0))
    return proj1(ends, rows, inners[2], w_proj, sends1, (low, high), out)[None]


def solution(mesh):
    placed = (
        P(("groups", "dp"), "seq", "chan"),
        P(("groups", "dp"), None),
        P(),
        P(None, None, None, "chan"),
        P(None, "chan", None),
        P(None, "chan"),
        P(None, "chan"),
    )
    return jax.shard_map(
        on_device,
        mesh=mesh,
        in_specs=placed,
        out_specs=P(("groups", "dp"), "seq", "chan"),
        check_vma=False,
    )
```

```python
import functools

import jax
import jax.numpy as jnp
from jax import lax
from jax.experimental import pallas as pl
from jax.experimental.pallas import tpu as pltpu
from jax.sharding import PartitionSpec as P

HALO = 64
EPS = 1e-05
F32 = jnp.float32
BF16 = jnp.bfloat16
SWAP = [(0, 1), (1, 0)]

ANY = pl.BlockSpec(memory_space=pl.ANY)
HBM = pl.BlockSpec(memory_space=pltpu.HBM)
INV = pl.BlockSpec(memory_space=pltpu.VMEM)
INS = pl.BlockSpec(memory_space=pltpu.SMEM)
FREE = pl.CostEstimate(flops=0, transcendentals=0, bytes_accessed=0)


def limit(mib):
    return pltpu.CompilerParams(vmem_limit_bytes=mib << 20)


dot = functools.partial(jnp.dot, preferred_element_type=F32)
copy = pltpu.make_async_copy


def shape(dims, dtype):
    return jax.ShapeDtypeStruct(tuple(dims), dtype)


def gelu(x):
    return jax.nn.gelu(x)


def side_of(back, n):
    return lax.rem(lax.axis_index("chan") - back + n, n)


def columns(back, n, width):
    return pl.ds(pl.multiple_of(side_of(back, n) * width, 128), width)


def run(copies):
    for c in copies:
        c.start()
    for c in copies:
        c.wait()


def sums_about(v, pivot):
    gap = (v - pivot).reshape(v.shape[0] // 8, 8, v.shape[1])
    return jnp.sum(gap, axis=0), jnp.sum(gap * gap, axis=0)


def spread_of(pivot, s1, s2, rows):
    s1 = jnp.sum(s1, axis=0, keepdims=True)
    s2 = jnp.sum(s2, axis=0, keepdims=True)
    off = s1 * (1.0 / rows)
    return pivot + off, s2 - s1 * off


def merged(a, b, n):
    gap = a[0:1] - b[0:1]
    return (a[0:1] + b[0:1]) * 0.5, a[1:2] + b[1:2] + gap * gap * (0.5 * n)


def pre_kernel(x_hbm, gains, biases, x, out, send1, send2, gains_out, biases_out, sems):
    rows = x.shape[0]
    load = copy(x_hbm, x, sems.at[2])
    load.start()
    copies = [copy(gains, gains_out, sems.at[0]), copy(biases, biases_out, sems.at[1])]
    for c in copies:
        c.start()
    load.wait()
    pivot = jnp.mean(x[0:16, :].astype(F32)[0:8], axis=0, keepdims=True)
    s1 = s2 = jnp.zeros((8, x.shape[1]), F32)
    for r in range(0, rows, 64):
        t1, t2 = sums_about(x[r : r + 64, :].astype(F32), pivot)
        s1, s2 = s1 + t1, s2 + t2
    out[0:1, :], out[1:2, :] = spread_of(pivot, s1, s2, rows)
    odd = lax.rem(lax.axis_index("seq"), 2)
    end = rows - HALO
    send1[...] = x[pl.ds(pl.multiple_of((1 - odd) * end, HALO), HALO), :]
    send2[...] = x[pl.ds(pl.multiple_of(odd * end, HALO), HALO), :]
    for c in copies:
        c.wait()


def pre(own, gains, biases):
    edge = shape((HALO, own.shape[1]), BF16)
    vector = shape(gains.shape, F32)
    return pl.pallas_call(
        pre_kernel,
        out_shape=(
            shape(own.shape, BF16),
            shape((2, own.shape[1]), F32),
            edge,
            edge,
            vector,
            vector,
        ),
        in_specs=[HBM] * 3,
        out_specs=(INV,) * 6,
        scratch_shapes=[pltpu.SemaphoreType.DMA((3,))],
        compiler_params=limit(4),
        cost_estimate=FREE,
        name="pre",
    )(own, gains, biases)


def merge_kernel(n, a, b, out):
    out[0:1, :], out[1:2, :] = merged(a[...], b[...], n)


def scale_of(m2, n, gain):
    return lax.rsqrt(m2 * (1.0 / n) + EPS) * gain


def finish0_kernel(n, a, b, gains, biases, *rest):
    out = rest[-1]
    mean, m2 = merged(a[...], b[...], n)
    out[0:1, :] = mean
    out[1:2, :] = scale_of(m2, 2 * n, gains[0:1, :])
    out[2:3, :] = biases[0:1, :]
    out[3:4, :] = gains[1:2, :]
    out[4:5, :] = biases[1:2, :]


def finish1_kernel(n, a, b, joined, *rest):
    out = rest[-1]
    mean, m2 = merged(a[...], b[...], n)
    out[0:1, :] = mean
    out[1:2, :] = scale_of(m2, 2 * n, joined[3:4, :])
    out[2:3, :] = joined[4:5, :]


def batch_stats(stat, n, kernel, extra, n_order):
    steps = []
    for axis in ("dp", "seq"):
        size, step = lax.axis_size(axis), 1
        while step < size:
            steps.append((axis, [(i, i ^ step) for i in range(size)]))
            step *= 2
    channels = stat.shape[1]
    found = []
    for at, (axis, pairs) in enumerate(steps):
        other = lax.ppermute(stat, axis, pairs)
        last = at == len(steps) - 1
        more = extra if last else ()
        stat = pl.pallas_call(
            functools.partial(kernel if last else merge_kernel, n),
            out_shape=shape((8 if last else 2, channels), F32),
            in_specs=[INV] * (2 + len(more) - (n_order if last else 0))
            + [ANY] * (n_order if last else 0),
            out_specs=INV,
            compiler_params=limit(1),
            cost_estimate=FREE,
            name="finish" if last else "merge",
        )(stat, other, *more)
        found.append(stat)
        n *= 2
    return found


def join_kernel(n, n_order, *refs):
    vecs, xs, (joined, send1, send2) = refs[:n], refs[n : 2 * n], refs[2 * n + n_order :]
    rows, width = xs[0].shape
    end = rows - HALO
    odd = lax.rem(lax.axis_index("seq"), 2)
    for k, (vec, x) in enumerate(zip(vecs, xs)):
        cols = columns(k, n, width)
        joined[:, cols] = vec[...]
        send1[:, cols] = x[pl.ds(pl.multiple_of((1 - odd) * end, HALO), HALO), :]
        send2[:, cols] = x[pl.ds(pl.multiple_of(odd * end, HALO), HALO), :]


def join(vecs, xs, order):
    n, width = len(vecs), vecs[0].shape[1]
    outs = [shape((8, n * width), F32)] + [shape((HALO, n * width), BF16)] * 2
    return pl.pallas_call(
        functools.partial(join_kernel, n, len(order)),
        out_shape=outs,
        in_specs=[INV] * (2 * n) + [ANY] * len(order),
        out_specs=[INV] * 3,
        compiler_params=limit(4),
        cost_estimate=FREE,
        name="join",
    )(*vecs, *xs, *order)


def cut_kernel(n, w, _, wsend, *rest):
    wsend1, sems = rest[:-1], rest[-1]
    core = lax.axis_index("dp")
    part = wsend.shape[0]
    quarter = lax.axis_index("groups") * 2 + core
    copies = [copy(w.at[0, pl.ds(pl.multiple_of(quarter * part, 16), part)], wsend, sems.at[0])]
    for k, dst in enumerate(wsend1):
        size, width = dst.shape
        mine = pl.ds(pl.multiple_of(core * size, 16), size)
        src = w.at[1, mine, columns(-k - 1, n, width)]
        copies.append(copy(src, dst, sems.at[k + 1]))
    run(copies)


def cut(w_proj, n, order):
    hidden, channels = w_proj.shape[1:]
    outs = [shape((hidden // 4, channels), BF16)]
    outs += [shape((hidden // 2, channels // n), BF16)] * (n - 1)
    return pl.pallas_call(
        functools.partial(cut_kernel, n),
        out_shape=outs,
        in_specs=[ANY, ANY],
        out_specs=[ANY] * n,
        scratch_shapes=[pltpu.SemaphoreType.DMA((n,))],
        compiler_params=limit(1),
        cost_estimate=FREE,
        name="cut",
    )(w_proj, order)


def keep_kernel(lengths_hbm, dilations_hbm, out, lengths, dilations, sems):
    rows = out.shape[1]
    run([copy(lengths_hbm, lengths, sems.at[0]), copy(dilations_hbm, dilations, sems.at[1])])
    first = lax.axis_index("seq") * rows
    ends, end = [], jnp.int32(0)
    for k in range(lengths.shape[1]):
        end = end + lengths[0, k]
        ends.append(end)

    def segment(place):
        count = jnp.where(place >= 0, 1, 0)
        for end in ends:
            count = count + jnp.where(place >= end, 1, 0)
        return count

    @pl.loop(0, rows // 32)
    def _(i):
        at = pl.multiple_of(i * 32, 32)
        place = first + at + lax.broadcasted_iota(jnp.int32, (32, 128), 0)
        here = segment(place)
        for layer in range(2):
            d = dilations[layer]
            for side, there in enumerate((place - d, place + d)):
                keep = jnp.where(segment(there) == here, 1.0, 0.0)
                out[2 * layer + side, pl.ds(at, 32), :] = keep


def keeps(lengths, dilations, rows):
    return pl.pallas_call(
        keep_kernel,
        out_shape=shape((4, rows, 128), F32),
        in_specs=[HBM, HBM],
        out_specs=INV,
        scratch_shapes=[
            pltpu.SMEM(lengths.shape, jnp.int32),
            pltpu.SMEM(dilations.shape, jnp.int32),
            pltpu.SemaphoreType.DMA((2,)),
        ],
        compiler_params=limit(4),
                cost_estimate=FREE,
                name="keeps",
    )(lengths, dilations)


def shifted(ref, start, count):
    base = pl.multiple_of((start // 8) * 8, 8)
    tall = ref[pl.ds(base, count + 8), :]
    return pltpu.roll(tall, (count + 8 - (start - base)) % (count + 8), 0)[:count]


def stage_kernel(w, *rest):
    layers, taps, _, width = w.shape
    outs, bufs, sems = rest[:layers], rest[layers:-1], rest[-1]
    step = outs[0].shape[1] // taps
    order = (0, 2, 1)
    copies = []
    for layer, out in enumerate(outs):
        for at, tap in enumerate(order):
            dst = bufs[0].at[layer, at] if bufs else out.at[:, pl.ds(at * step, width)]
            copies.append(copy(w.at[layer, tap], dst, sems.at[len(copies)]))
    run(copies)
    for buf in bufs:
        for layer, out in enumerate(outs):
            for at in range(taps):
                out[:, at * step : at * step + width] = buf[layer, at]


def stage(w_conv):
    layers, taps, channels, width = w_conv.shape
    step = -(-width // 128) * 128
    bufs = [] if step == width else [pltpu.VMEM(w_conv.shape, BF16)]
    return pl.pallas_call(
        stage_kernel,
        out_shape=[shape((channels, taps * step), BF16)] * layers,
        in_specs=[HBM],
        out_specs=[INV] * layers,
        scratch_shapes=bufs + [pltpu.SemaphoreType.DMA((layers * taps,))],
        compiler_params=limit(8 if bufs else 1),
        cost_estimate=FREE,
        name="stage",
    )(w_conv)


def conv_kernel(pieces, layer, segs, hand, n, n_src, n_order, dilations_hbm, stats, keep, w, *rest):
    srcs, rest = rest[:n_src], rest[n_src + n_order :]
    out, *kept, nbuf, p0, p2, dilations, sem = rest
    load = copy(dilations_hbm, dilations, sem)
    load.start()
    ext, width = nbuf.shape[0], out.shape[1]
    for src, at, count, to, back, raw in pieces:
        src = srcs[src]
        cols = slice(None) if back is None else columns(back, n, src.shape[1])
        if isinstance(to, tuple):
            odd = lax.rem(lax.axis_index("seq"), 2)
            to = pl.multiple_of(to[0] + odd * (to[1] - to[0]), HALO)
        if not raw:
            nbuf[to : to + count, cols] = src[at : at + count, :]
            continue
        mean, scale, bias = stats[0:1, cols], stats[1:2, cols], stats[2:3, cols]
        block = 128 if count % 128 == 0 else 64

        for rows in range(0, count, block):
            v = src[at + rows : at + rows + block, :].astype(F32)
            dst = pl.ds(pl.multiple_of(to + rows, HALO), block)
            nbuf[dst, cols] = gelu((v - mean) * scale + bias).astype(BF16)

    step = w.shape[1] // 3
    sides = dot(nbuf[...], w[:, : 2 * step])
    p0[0 : ext - HALO, :] = sides[: ext - HALO, :width]
    p2[0 : ext - HALO, :] = sides[HALO:, step : step + width]
    mid = dot(nbuf[HALO : ext - HALO, :], w[:, 2 * step : 2 * step + width])
    load.wait()
    d = dilations[layer]
    to = 0
    for k, (first, count) in enumerate(segs):
        base = to + 2 * HALO * k
        for r in range(0, count, HALO):
            left = shifted(p0, base + r + HALO - d, HALO)
            right = shifted(p2, base + r + d, HALO)
            here = slice(first + r, first + r + HALO)
            for c in range(0, width, 128):
                wide = min(128, width - c)
                cs = slice(c, c + wide)
                kl, kr = keep[2 * layer, here, :wide] > 0, keep[2 * layer + 1, here, :wide] > 0
                mixed = jnp.where(kl, left[:, cs], 0.0) + jnp.where(kr, right[:, cs], 0.0)
                mixed = mid[base + r : base + r + HALO, cs] + mixed
                out[to + r : to + r + HALO, cs] = gelu(mixed).astype(BF16)
        to += count
    for ref in kept:
        ref[...] = nbuf[hand : hand + 2 * HALO, :]


def conv(pieces, srcs, n, layer, segs, dilations, stats, keep, w, width, order, hand=None):
    channels = w.shape[0]
    rows = sum(count for _, count in segs)
    ext = rows + 2 * HALO * len(segs)
    outs = [shape((rows, width), BF16)]
    outs += [shape((2 * HALO, channels), BF16)] * int(hand is not None)
    cost = pl.CostEstimate(flops=0, transcendentals=0, bytes_accessed=24 << 20)
    return pl.pallas_call(
        functools.partial(conv_kernel, pieces, layer, segs, hand, n, len(srcs), len(order)),
        out_shape=outs,
        in_specs=[HBM] + [INV] * (3 + len(srcs)) + [ANY] * len(order),
        out_specs=[INV] * len(outs),
        scratch_shapes=[
            pltpu.VMEM((ext, channels), BF16),
            pltpu.VMEM((ext - HALO + 8, width), F32),
            pltpu.VMEM((ext - HALO + 8, width), F32),
            pltpu.SMEM(dilations.shape, jnp.int32),
            pltpu.SemaphoreType.DMA,
        ],
        compiler_params=limit(10),
        cost_estimate=cost,
        name=f"conv{layer}_{segs[0][0]}",
    )(dilations, stats, keep, w, *srcs, *order)


def weight_copies(sends, wbuf, sems):
    copies = []
    for k, parts in enumerate(sends):
        size = parts[0][0].shape[0]
        for src, at in parts:
            dst = wbuf.at[k, pl.ds(pl.multiple_of(at * size, 16), size), :]
            copies.append(copy(src, dst, sems.at[len(copies)]))
    return copies


def quarters(refs):
    group, core = lax.axis_index("groups"), lax.axis_index("dp")
    ats = (2 * group + core, 2 * (1 - group) + core, 2 * group + 1 - core, 3 - 2 * group - core)
    return [list(zip(refs[i : i + 4], ats)) for i in range(0, len(refs), 4)]


def halves(refs):
    core = lax.axis_index("dp")
    return [list(zip(refs[i : i + 2], (core, 1 - core))) for i in range(0, len(refs), 2)]


def update_of(inners, w, layer, cols, wbuf, others):
    total = dot(inners[0][...], w[layer, :, cols]).astype(BF16).astype(F32)
    for k, inner in enumerate(inners[1:]):
        total = total + dot(inner[...], wbuf[k, :, others]).astype(BF16).astype(F32)
    return total


def proj0_kernel(n, runs, *rest):
    chunks = [rest[i * n : (i + 1) * n] for i in range(len(runs))]
    rest = rest[len(runs) * n :]
    w, sends, rest = rest[0], rest[1 : 4 * n - 3], rest[4 * n - 3 :]
    xs, (mid, low, high, send1, send2, stat, wbuf, wsems) = rest[:n], rest[n:]
    rows, width = xs[0].shape
    end = rows - HALO
    run(weight_copies(quarters(sends), wbuf, wsems))
    even = lax.rem(lax.axis_index("seq"), 2) == 0
    for k, x in enumerate(xs):
        for col in range(0, width, 256):
            wide = min(256, width - col)
            here = slice(col, col + wide)
            cs = pl.ds(pl.multiple_of(side_of(k, n) * width + col, 128), wide)
            pivot, edge = None, {}
            for chunk, spans in zip(chunks, runs):
                update = update_of(chunk, w, 0, cs, wbuf, cs)
                at = 0
                for first, count in spans:
                    new = x[first : first + count, here].astype(F32) + update[at : at + count]
                    new = new.astype(BF16)
                    v = new.astype(F32)
                    if first in (0, end):
                        edge[first] = v
                        (high if first else low)[:, cs] = new
                    else:
                        mid[first - HALO : first - HALO + count, cs] = new
                    if pivot is None:
                        pivot = jnp.mean(v[0:8], axis=0, keepdims=True)
                        s1 = s2 = jnp.zeros((8, wide), F32)
                    t1, t2 = sums_about(v, pivot)
                    s1, s2 = s1 + t1, s2 + t2
                    at += count
            send1[:, cs] = jnp.where(even, edge[end], edge[0]).astype(BF16)
            send2[:, cs] = jnp.where(even, edge[0], edge[end]).astype(BF16)
            stat[0:1, cs], stat[1:2, cs] = spread_of(pivot, s1, s2, rows)


def proj0(runs, inners, w_proj, sends, xs):
    hidden, channels = w_proj.shape[1:]
    n = len(xs)
    rows = xs[0].shape[0]
    outs = [shape((rows - 2 * HALO, channels), BF16)]
    outs += [shape((HALO, channels), BF16)] * 4 + [shape((2, channels), F32)]
    return pl.pallas_call(
        functools.partial(proj0_kernel, n, runs),
        out_shape=outs,
        in_specs=[INV] * (len(runs) * n + 1) + [ANY] * len(sends) + [INV] * n,
        out_specs=[INV] * 6,
        scratch_shapes=[
            pltpu.VMEM((n - 1, hidden, channels), BF16),
            pltpu.SemaphoreType.DMA((4 * n - 4,)),
        ],
        compiler_params=limit(8),
        cost_estimate=FREE,
        name="proj0",
    )(*[x for chunk in inners for x in chunk], w_proj, *sends, *xs)


def proj1_kernel(runs, n, n_src, last, *rest):
    inners, w, sends, rest = rest[:n], rest[n], rest[n + 1 : 3 * n - 1], rest[3 * n - 1 :]
    srcs, (out, obuf, wbuf, sems, wsems) = rest[:n_src], rest[n_src + int(last) :]
    width = obuf.shape[1]
    run(weight_copies(halves(sends), wbuf, wsems))
    for col in range(0, width, 256):
        wide = min(256, width - col)
        here = slice(col, col + wide)
        cs = pl.ds(pl.multiple_of(side_of(0, n) * width + col, 128), wide)
        update = update_of(inners, w, 1, cs, wbuf, here)
        at = 0
        for (_, count, skip), src in zip(runs, srcs):
            new = src[skip : skip + count, cs].astype(F32) + update[at : at + count]
            obuf[at : at + count, here] = new.astype(BF16)
            at += count
    at, outs = 0, []
    for k, (first, count, _) in enumerate(runs):
        outs.append(copy(obuf.at[pl.ds(at, count)], out.at[pl.ds(first, count)], sems.at[k]))
        at += count
    run(outs)


def proj1(runs, total, inners, w_proj, sends, srcs, before=None):
    hidden, channels = w_proj.shape[1:]
    n = len(inners)
    width = channels // n
    rows = sum(count for _, count, _ in runs)
    last = before is not None
    extra = [before] if last else []
    return pl.pallas_call(
        functools.partial(proj1_kernel, runs, n, len(srcs), last),
        out_shape=shape((total, width), BF16),
        in_specs=[INV] * (n + 1)
        + [ANY] * len(sends)
        + [INV] * len(srcs)
        + [HBM] * len(extra),
        out_specs=HBM,
        scratch_shapes=[
            pltpu.VMEM((rows, width), BF16),
            pltpu.VMEM((n - 1, hidden, width), BF16),
            pltpu.SemaphoreType.DMA((len(runs),)),
            pltpu.SemaphoreType.DMA((2 * n - 2,)),
        ],
        input_output_aliases={n + 1 + len(sends) + len(srcs): 0} if last else {},
        compiler_params=limit(5),
        cost_estimate=FREE,
        name=f"proj1_{runs[0][0]}",
    )(*inners, w_proj, *sends, *srcs, *extra)


def on_device(signal, lengths, dilations, w_conv, w_proj, gains, biases):
    own = signal[0]
    rows = own.shape[0]
    width = w_conv.shape[3]
    end = rows - HALO
    n_seq, n = lax.axis_size("seq"), lax.axis_size("chan")
    pairs1 = [(i, i ^ 1) for i in range(n_seq)]
    pairs2 = [(i, i + 1 if i % 2 else i - 1) for i in range(1, n_seq - 1)]
    perm = lax.ppermute
    pinned = pltpu.with_memory_space_constraint
    tied = lax.optimization_barrier

    def others(value):
        return [perm(value, "chan", [(i, (i + k) % n) for i in range(n)]) for k in range(1, n)]

    sent = others(own)
    own = pinned(own, pltpu.HBM)
    taps = [pinned(w, pltpu.VMEM) for w in stage(pinned(w_conv, pltpu.HBM))]
    lengths, dilations = pinned(lengths, pltpu.HBM), pinned(dilations, pltpu.HBM)
    keep = pinned(keeps(lengths, dilations, rows), pltpu.VMEM)
    gains, biases = pinned(gains, pltpu.HBM), pinned(biases, pltpu.HBM)
    own, stat, _, _, gains, biases = pre(own, gains, biases)
    xs = [pinned(own, pltpu.VMEM)] + [pinned(x, pltpu.VMEM) for x in sent]
    found = batch_stats(stat, rows, finish0_kernel, (gains, biases, keep), 1)
    w_proj = pinned(w_proj, pltpu.VMEM)
    vecs = [found[-1]]
    for k in range(1, n):
        pairs = []
        for z in range(n_seq):
            for c in range(n):
                pairs.append((z * n + c, (z ^ 1) * n + (c + k) % n))
        vecs.append(perm(found[-1], ("seq", "chan"), pairs))
    wsend, *wsend1 = cut(w_proj, n, found[-1])
    sent = others(wsend)
    joined, send1, send2 = join(vecs, xs, taps)

    half = rows // 2
    runs = (((HALO, half - HALO),), ((half, half - HALO),), ((0, HALO), (end, HALO)))
    at1, at2 = (5 * HALO, 0), (0, 5 * HALO)

    def inner_rows(layer, chunk, pieces, srcs, stats, *order):
        hand = chunk * (half - HALO)
        return conv(
            pieces,
            srcs,
            n,
            layer,
            runs[chunk],
            dilations,
            stats,
            keep,
            taps[layer],
            width,
            order,
            hand,
        )

    def edge_rows(layer, kept, halos, stats, *order):
        pieces = [(0, 0, 2 * HALO, HALO, None, False), (1, 0, 2 * HALO, 3 * HALO, None, False)]
        srcs = list(kept)
        for halo, at in zip(halos, (at1, at2)):
            pieces += [(len(srcs), 0, HALO, at, None, True)]
            srcs += [halo]
        return conv(
            pieces, srcs, n, layer, runs[2], dilations, stats, keep, taps[layer], width, order
        )[0]

    tall = half + HALO
    pieces_a = [(k, 0, tall, 0, k, True) for k in range(n)]
    pieces_b = [(k, half - HALO, tall, 0, k, True) for k in range(n)]
    inner_a, kept_a = inner_rows(0, 0, pieces_a, xs, joined)
    send1, send2, sent, inner_a = tied((send1, send2, sent, inner_a))
    halos = perm(send1, "seq", pairs1), perm(send2, "seq", pairs2)
    swapped = [perm(w, "groups", SWAP) for w in sent]
    others_a = others(inner_a)
    inner_b, kept_b = inner_rows(0, 1, pieces_b, xs, joined, kept_a)
    swapped, inner_b = tied((swapped, inner_b))
    inner_c = edge_rows(0, (kept_a, kept_b), halos, joined, *others_a)
    sends0 = []
    for w, w2 in zip(sent, swapped):
        sends0 += [w, w2, perm(w, "dp", SWAP), perm(w2, "dp", SWAP)]
    inners = [[inner_a] + others_a] + [[inner] + others(inner) for inner in (inner_b, inner_c)]
    mid, low, high, send1, send2, stat = proj0(runs, inners, w_proj, sends0, xs)
    found = batch_stats(stat, rows, finish1_kernel, (joined,), 0)
    stats1 = found[-1]
    wsend1, _ = tied((wsend1, found[0]))
    sends1 = []
    for k, w in enumerate(wsend1):
        w = perm(w, "chan", [(i, (i + k + 1) % n) for i in range(n)])
        sends1 += [w, perm(w, "dp", SWAP)]
    send1, send2, _ = tied((send1, send2, stats1))
    halos = perm(send1, "seq", pairs1), perm(send2, "seq", pairs2)

    pieces_a = ((0, 0, HALO, 0, None, True), (1, 0, half, HALO, None, True))
    pieces_b = (
        (1, half - 2 * HALO, half, 0, None, True),
        (2, 0, HALO, half, None, True),
    )
    inner_a, kept_a = inner_rows(1, 0, pieces_a, (low, mid), stats1)
    inner_b, kept_b = inner_rows(1, 1, pieces_b, (low, mid, high), stats1, kept_a)
    inner_c = edge_rows(1, (kept_a, kept_b), halos, stats1)
    inners = [[inner] + others(inner) for inner in (inner_a, inner_b, inner_c)]
    out = proj1(((HALO, half - HALO, 0),), rows, inners[0], w_proj, sends1, (mid,))
    out = proj1(((half, half - HALO, half - HALO),), rows, inners[1], w_proj, sends1, (mid,), out)
    ends = ((0, HALO, 0), (end, HALO, 0))
    return proj1(ends, rows, inners[2], w_proj, sends1, (low, high), out)[None]


def solution(mesh):
    placed = (
        P(("groups", "dp"), "seq", "chan"),
        P(("groups", "dp"), None),
        P(),
        P(None, None, None, "chan"),
        P(None, "chan", None),
        P(None, "chan"),
        P(None, "chan"),
    )
    return jax.shard_map(
        on_device,
        mesh=mesh,
        in_specs=placed,
        out_specs=P(("groups", "dp"), "seq", "chan"),
        check_vma=False,
    )
```

```python
import functools

import jax
import jax.numpy as jnp
from jax import lax
from jax.experimental import pallas as pl
from jax.experimental.pallas import tpu as pltpu
from jax.sharding import PartitionSpec as P

HALO = 64
EPS = 1e-05
F32 = jnp.float32
BF16 = jnp.bfloat16
SWAP = [(0, 1), (1, 0)]

ANY = pl.BlockSpec(memory_space=pl.ANY)
HBM = pl.BlockSpec(memory_space=pltpu.HBM)
INV = pl.BlockSpec(memory_space=pltpu.VMEM)
INS = pl.BlockSpec(memory_space=pltpu.SMEM)
FREE = pl.CostEstimate(flops=0, transcendentals=0, bytes_accessed=0)


def limit(mib):
    return pltpu.CompilerParams(vmem_limit_bytes=mib << 20)


dot = functools.partial(jnp.dot, preferred_element_type=F32)
copy = pltpu.make_async_copy


def shape(dims, dtype):
    return jax.ShapeDtypeStruct(tuple(dims), dtype)


def gelu(x):
    return jax.nn.gelu(x)


def side_of(back, n):
    return lax.rem(lax.axis_index("chan") - back + n, n)


def columns(back, n, width):
    return pl.ds(pl.multiple_of(side_of(back, n) * width, 128), width)


def run(copies):
    for c in copies:
        c.start()
    for c in copies:
        c.wait()


def sums_about(v, pivot):
    gap = (v - pivot).reshape(v.shape[0] // 8, 8, v.shape[1])
    return jnp.sum(gap, axis=0), jnp.sum(gap * gap, axis=0)


def spread_of(pivot, s1, s2, rows):
    s1 = jnp.sum(s1, axis=0, keepdims=True)
    s2 = jnp.sum(s2, axis=0, keepdims=True)
    off = s1 * (1.0 / rows)
    return pivot + off, s2 - s1 * off


def merged(a, b, n):
    gap = a[0:1] - b[0:1]
    return (a[0:1] + b[0:1]) * 0.5, a[1:2] + b[1:2] + gap * gap * (0.5 * n)


def pre_kernel(x_hbm, gains, biases, x, out, send1, send2, gains_out, biases_out, sems):
    rows = x.shape[0]
    load = copy(x_hbm, x, sems.at[2])
    load.start()
    copies = [copy(gains, gains_out, sems.at[0]), copy(biases, biases_out, sems.at[1])]
    for c in copies:
        c.start()
    load.wait()
    pivot = jnp.mean(x[0:16, :].astype(F32)[0:8], axis=0, keepdims=True)
    s1 = s2 = jnp.zeros((8, x.shape[1]), F32)
    for r in range(0, rows, 64):
        t1, t2 = sums_about(x[r : r + 64, :].astype(F32), pivot)
        s1, s2 = s1 + t1, s2 + t2
    out[0:1, :], out[1:2, :] = spread_of(pivot, s1, s2, rows)
    odd = lax.rem(lax.axis_index("seq"), 2)
    end = rows - HALO
    send1[...] = x[pl.ds(pl.multiple_of((1 - odd) * end, HALO), HALO), :]
    send2[...] = x[pl.ds(pl.multiple_of(odd * end, HALO), HALO), :]
    for c in copies:
        c.wait()


def pre(own, gains, biases):
    edge = shape((HALO, own.shape[1]), BF16)
    vector = shape(gains.shape, F32)
    return pl.pallas_call(
        pre_kernel,
        out_shape=(
            shape(own.shape, BF16),
            shape((2, own.shape[1]), F32),
            edge,
            edge,
            vector,
            vector,
        ),
        in_specs=[HBM] * 3,
        out_specs=(INV,) * 6,
        scratch_shapes=[pltpu.SemaphoreType.DMA((3,))],
        compiler_params=limit(4),
        cost_estimate=FREE,
        name="pre",
    )(own, gains, biases)


def merge_kernel(n, a, b, out):
    out[0:1, :], out[1:2, :] = merged(a[...], b[...], n)


def scale_of(m2, n, gain):
    return lax.rsqrt(m2 * (1.0 / n) + EPS) * gain


def finish0_kernel(n, a, b, gains, biases, *rest):
    out = rest[-1]
    mean, m2 = merged(a[...], b[...], n)
    out[0:1, :] = mean
    out[1:2, :] = scale_of(m2, 2 * n, gains[0:1, :])
    out[2:3, :] = biases[0:1, :]
    out[3:4, :] = gains[1:2, :]
    out[4:5, :] = biases[1:2, :]


def finish1_kernel(n, a, b, joined, *rest):
    out = rest[-1]
    mean, m2 = merged(a[...], b[...], n)
    out[0:1, :] = mean
    out[1:2, :] = scale_of(m2, 2 * n, joined[3:4, :])
    out[2:3, :] = joined[4:5, :]


def batch_stats(stat, n, kernel, extra, n_order):
    steps = []
    for axis in ("dp", "seq"):
        size, step = lax.axis_size(axis), 1
        while step < size:
            steps.append((axis, [(i, i ^ step) for i in range(size)]))
            step *= 2
    channels = stat.shape[1]
    found = []
    for at, (axis, pairs) in enumerate(steps):
        other = lax.ppermute(stat, axis, pairs)
        last = at == len(steps) - 1
        more = extra if last else ()
        stat = pl.pallas_call(
            functools.partial(kernel if last else merge_kernel, n),
            out_shape=shape((8 if last else 2, channels), F32),
            in_specs=[INV] * (2 + len(more) - (n_order if last else 0))
            + [ANY] * (n_order if last else 0),
            out_specs=INV,
            compiler_params=limit(1),
            cost_estimate=FREE,
            name="finish" if last else "merge",
        )(stat, other, *more)
        found.append(stat)
        n *= 2
    return found


def join_kernel(n, n_order, *refs):
    vecs, xs, (joined, send1, send2) = refs[:n], refs[n : 2 * n], refs[2 * n + n_order :]
    rows, width = xs[0].shape
    end = rows - HALO
    odd = lax.rem(lax.axis_index("seq"), 2)
    for k, (vec, x) in enumerate(zip(vecs, xs)):
        cols = columns(k, n, width)
        joined[:, cols] = vec[...]
        send1[:, cols] = x[pl.ds(pl.multiple_of((1 - odd) * end, HALO), HALO), :]
        send2[:, cols] = x[pl.ds(pl.multiple_of(odd * end, HALO), HALO), :]


def join(vecs, xs, order):
    n, width = len(vecs), vecs[0].shape[1]
    outs = [shape((8, n * width), F32)] + [shape((HALO, n * width), BF16)] * 2
    return pl.pallas_call(
        functools.partial(join_kernel, n, len(order)),
        out_shape=outs,
        in_specs=[INV] * (2 * n) + [ANY] * len(order),
        out_specs=[INV] * 3,
        compiler_params=limit(4),
        cost_estimate=FREE,
        name="join",
    )(*vecs, *xs, *order)


def cut_kernel(n, w, _, wsend, *rest):
    wsend1, sems = rest[:-1], rest[-1]
    core = lax.axis_index("dp")
    part = wsend.shape[0]
    quarter = lax.axis_index("groups") * 2 + core
    copies = [copy(w.at[0, pl.ds(pl.multiple_of(quarter * part, 16), part)], wsend, sems.at[0])]
    for k, dst in enumerate(wsend1):
        size, width = dst.shape
        mine = pl.ds(pl.multiple_of(core * size, 16), size)
        src = w.at[1, mine, columns(-k - 1, n, width)]
        copies.append(copy(src, dst, sems.at[k + 1]))
    run(copies)


def cut(w_proj, n, order):
    hidden, channels = w_proj.shape[1:]
    outs = [shape((hidden // 4, channels), BF16)]
    outs += [shape((hidden // 2, channels // n), BF16)] * (n - 1)
    return pl.pallas_call(
        functools.partial(cut_kernel, n),
        out_shape=outs,
        in_specs=[ANY, ANY],
        out_specs=[ANY] * n,
        scratch_shapes=[pltpu.SemaphoreType.DMA((n,))],
        compiler_params=limit(1),
        cost_estimate=FREE,
        name="cut",
    )(w_proj, order)


def keep_kernel(lengths_hbm, dilations_hbm, out, lengths, dilations, sems):
    rows = out.shape[1]
    run([copy(lengths_hbm, lengths, sems.at[0]), copy(dilations_hbm, dilations, sems.at[1])])
    first = lax.axis_index("seq") * rows
    ends, end = [], jnp.int32(0)
    for k in range(lengths.shape[1]):
        end = end + lengths[0, k]
        ends.append(end)

    def segment(place):
        count = jnp.where(place >= 0, 1, 0)
        for end in ends:
            count = count + jnp.where(place >= end, 1, 0)
        return count

    @pl.loop(0, rows // 32)
    def _(i):
        at = pl.multiple_of(i * 32, 32)
        place = first + at + lax.broadcasted_iota(jnp.int32, (32, 128), 0)
        here = segment(place)
        for layer in range(2):
            d = dilations[layer]
            for side, there in enumerate((place - d, place + d)):
                keep = jnp.where(segment(there) == here, 1.0, 0.0)
                out[2 * layer + side, pl.ds(at, 32), :] = keep


def keeps(lengths, dilations, rows):
    return pl.pallas_call(
        keep_kernel,
        out_shape=shape((4, rows, 128), F32),
        in_specs=[HBM, HBM],
        out_specs=INV,
        scratch_shapes=[
            pltpu.SMEM(lengths.shape, jnp.int32),
            pltpu.SMEM(dilations.shape, jnp.int32),
            pltpu.SemaphoreType.DMA((2,)),
        ],
        compiler_params=limit(4),
                cost_estimate=FREE,
                name="keeps",
    )(lengths, dilations)


def shifted(ref, start, count):
    base = pl.multiple_of((start // 8) * 8, 8)
    tall = ref[pl.ds(base, count + 8), :]
    return pltpu.roll(tall, (count + 8 - (start - base)) % (count + 8), 0)[:count]


def stage_kernel(w, *rest):
    layers, taps, _, width = w.shape
    outs, bufs, sems = rest[:layers], rest[layers:-1], rest[-1]
    step = outs[0].shape[1] // taps
    order = (0, 2, 1)
    copies = []
    for layer, out in enumerate(outs):
        for at, tap in enumerate(order):
            dst = bufs[0].at[layer, at] if bufs else out.at[:, pl.ds(at * step, width)]
            copies.append(copy(w.at[layer, tap], dst, sems.at[len(copies)]))
    run(copies)
    for buf in bufs:
        for layer, out in enumerate(outs):
            for at in range(taps):
                out[:, at * step : at * step + width] = buf[layer, at]


def stage(w_conv):
    layers, taps, channels, width = w_conv.shape
    step = -(-width // 128) * 128
    bufs = [] if step == width else [pltpu.VMEM(w_conv.shape, BF16)]
    return pl.pallas_call(
        stage_kernel,
        out_shape=[shape((channels, taps * step), BF16)] * layers,
        in_specs=[HBM],
        out_specs=[INV] * layers,
        scratch_shapes=bufs + [pltpu.SemaphoreType.DMA((layers * taps,))],
        compiler_params=limit(8 if bufs else 1),
        cost_estimate=FREE,
        name="stage",
    )(w_conv)


def conv_kernel(pieces, layer, segs, hand, n, n_src, n_order, dilations_hbm, stats, keep, w, *rest):
    srcs, rest = rest[:n_src], rest[n_src + n_order :]
    out, *kept, nbuf, p0, p2, dilations, sem = rest
    load = copy(dilations_hbm, dilations, sem)
    load.start()
    ext, width = nbuf.shape[0], out.shape[1]
    for src, at, count, to, back, raw in pieces:
        src = srcs[src]
        cols = slice(None) if back is None else columns(back, n, src.shape[1])
        if isinstance(to, tuple):
            odd = lax.rem(lax.axis_index("seq"), 2)
            to = pl.multiple_of(to[0] + odd * (to[1] - to[0]), HALO)
        if not raw:
            nbuf[to : to + count, cols] = src[at : at + count, :]
            continue
        mean, scale, bias = stats[0:1, cols], stats[1:2, cols], stats[2:3, cols]
        block = 32

        for rows in range(0, count, block):
            v = src[at + rows : at + rows + block, :].astype(F32)
            dst = pl.ds(pl.multiple_of(to + rows, 32), block)
            nbuf[dst, cols] = gelu((v - mean) * scale + bias).astype(BF16)

    step = w.shape[1] // 3
    sides = dot(nbuf[...], w[:, : 2 * step])
    p0[0 : ext - HALO, :] = sides[: ext - HALO, :width]
    p2[0 : ext - HALO, :] = sides[HALO:, step : step + width]
    mid = dot(nbuf[HALO : ext - HALO, :], w[:, 2 * step : 2 * step + width])
    load.wait()
    d = dilations[layer]
    to = 0
    for k, (first, count) in enumerate(segs):
        base = to + 2 * HALO * k
        for r in range(0, count, HALO):
            left = shifted(p0, base + r + HALO - d, HALO)
            right = shifted(p2, base + r + d, HALO)
            here = slice(first + r, first + r + HALO)
            for c in range(0, width, 128):
                wide = min(128, width - c)
                cs = slice(c, c + wide)
                kl, kr = keep[2 * layer, here, :wide] > 0, keep[2 * layer + 1, here, :wide] > 0
                mixed = jnp.where(kl, left[:, cs], 0.0) + jnp.where(kr, right[:, cs], 0.0)
                mixed = mid[base + r : base + r + HALO, cs] + mixed
                out[to + r : to + r + HALO, cs] = gelu(mixed).astype(BF16)
        to += count
    for ref in kept:
        ref[...] = nbuf[hand : hand + 2 * HALO, :]


def conv(pieces, srcs, n, layer, segs, dilations, stats, keep, w, width, order, hand=None):
    channels = w.shape[0]
    rows = sum(count for _, count in segs)
    ext = rows + 2 * HALO * len(segs)
    outs = [shape((rows, width), BF16)]
    outs += [shape((2 * HALO, channels), BF16)] * int(hand is not None)
    cost = pl.CostEstimate(flops=0, transcendentals=0, bytes_accessed=24 << 20)
    return pl.pallas_call(
        functools.partial(conv_kernel, pieces, layer, segs, hand, n, len(srcs), len(order)),
        out_shape=outs,
        in_specs=[HBM] + [INV] * (3 + len(srcs)) + [ANY] * len(order),
        out_specs=[INV] * len(outs),
        scratch_shapes=[
            pltpu.VMEM((ext, channels), BF16),
            pltpu.VMEM((ext - HALO + 8, width), F32),
            pltpu.VMEM((ext - HALO + 8, width), F32),
            pltpu.SMEM(dilations.shape, jnp.int32),
            pltpu.SemaphoreType.DMA,
        ],
        compiler_params=limit(10),
        cost_estimate=cost,
        name=f"conv{layer}_{segs[0][0]}",
    )(dilations, stats, keep, w, *srcs, *order)


def weight_copies(sends, wbuf, sems):
    copies = []
    for k, parts in enumerate(sends):
        size = parts[0][0].shape[0]
        for src, at in parts:
            dst = wbuf.at[k, pl.ds(pl.multiple_of(at * size, 16), size), :]
            copies.append(copy(src, dst, sems.at[len(copies)]))
    return copies


def quarters(refs):
    group, core = lax.axis_index("groups"), lax.axis_index("dp")
    ats = (2 * group + core, 2 * (1 - group) + core, 2 * group + 1 - core, 3 - 2 * group - core)
    return [list(zip(refs[i : i + 4], ats)) for i in range(0, len(refs), 4)]


def halves(refs):
    core = lax.axis_index("dp")
    return [list(zip(refs[i : i + 2], (core, 1 - core))) for i in range(0, len(refs), 2)]


def update_of(inners, w, layer, cols, wbuf, others):
    total = dot(inners[0][...], w[layer, :, cols]).astype(BF16).astype(F32)
    for k, inner in enumerate(inners[1:]):
        total = total + dot(inner[...], wbuf[k, :, others]).astype(BF16).astype(F32)
    return total


def proj0_kernel(n, runs, *rest):
    chunks = [rest[i * n : (i + 1) * n] for i in range(len(runs))]
    rest = rest[len(runs) * n :]
    w, sends, rest = rest[0], rest[1 : 4 * n - 3], rest[4 * n - 3 :]
    xs, (mid, low, high, send1, send2, stat, wbuf, wsems) = rest[:n], rest[n:]
    rows, width = xs[0].shape
    end = rows - HALO
    run(weight_copies(quarters(sends), wbuf, wsems))
    even = lax.rem(lax.axis_index("seq"), 2) == 0
    for k, x in enumerate(xs):
        for col in range(0, width, 256):
            wide = min(256, width - col)
            here = slice(col, col + wide)
            cs = pl.ds(pl.multiple_of(side_of(k, n) * width + col, 128), wide)
            pivot, edge = None, {}
            for chunk, spans in zip(chunks, runs):
                update = update_of(chunk, w, 0, cs, wbuf, cs)
                at = 0
                for first, count in spans:
                    new = x[first : first + count, here].astype(F32) + update[at : at + count]
                    new = new.astype(BF16)
                    v = new.astype(F32)
                    if first in (0, end):
                        edge[first] = v
                        (high if first else low)[:, cs] = new
                    else:
                        mid[first - HALO : first - HALO + count, cs] = new
                    if pivot is None:
                        pivot = jnp.mean(v[0:8], axis=0, keepdims=True)
                        s1 = s2 = jnp.zeros((8, wide), F32)
                    t1, t2 = sums_about(v, pivot)
                    s1, s2 = s1 + t1, s2 + t2
                    at += count
            send1[:, cs] = jnp.where(even, edge[end], edge[0]).astype(BF16)
            send2[:, cs] = jnp.where(even, edge[0], edge[end]).astype(BF16)
            stat[0:1, cs], stat[1:2, cs] = spread_of(pivot, s1, s2, rows)


def proj0(runs, inners, w_proj, sends, xs):
    hidden, channels = w_proj.shape[1:]
    n = len(xs)
    rows = xs[0].shape[0]
    outs = [shape((rows - 2 * HALO, channels), BF16)]
    outs += [shape((HALO, channels), BF16)] * 4 + [shape((2, channels), F32)]
    return pl.pallas_call(
        functools.partial(proj0_kernel, n, runs),
        out_shape=outs,
        in_specs=[INV] * (len(runs) * n + 1) + [ANY] * len(sends) + [INV] * n,
        out_specs=[INV] * 6,
        scratch_shapes=[
            pltpu.VMEM((n - 1, hidden, channels), BF16),
            pltpu.SemaphoreType.DMA((4 * n - 4,)),
        ],
        compiler_params=limit(8),
        cost_estimate=FREE,
        name="proj0",
    )(*[x for chunk in inners for x in chunk], w_proj, *sends, *xs)


def proj1_kernel(runs, n, n_src, last, *rest):
    inners, w, sends, rest = rest[:n], rest[n], rest[n + 1 : 3 * n - 1], rest[3 * n - 1 :]
    srcs, (out, obuf, wbuf, sems, wsems) = rest[:n_src], rest[n_src + int(last) :]
    width = obuf.shape[1]
    run(weight_copies(halves(sends), wbuf, wsems))
    for col in range(0, width, 256):
        wide = min(256, width - col)
        here = slice(col, col + wide)
        cs = pl.ds(pl.multiple_of(side_of(0, n) * width + col, 128), wide)
        update = update_of(inners, w, 1, cs, wbuf, here)
        at = 0
        for (_, count, skip), src in zip(runs, srcs):
            new = src[skip : skip + count, cs].astype(F32) + update[at : at + count]
            obuf[at : at + count, here] = new.astype(BF16)
            at += count
    at, outs = 0, []
    for k, (first, count, _) in enumerate(runs):
        outs.append(copy(obuf.at[pl.ds(at, count)], out.at[pl.ds(first, count)], sems.at[k]))
        at += count
    run(outs)


def proj1(runs, total, inners, w_proj, sends, srcs, before=None):
    hidden, channels = w_proj.shape[1:]
    n = len(inners)
    width = channels // n
    rows = sum(count for _, count, _ in runs)
    last = before is not None
    extra = [before] if last else []
    return pl.pallas_call(
        functools.partial(proj1_kernel, runs, n, len(srcs), last),
        out_shape=shape((total, width), BF16),
        in_specs=[INV] * (n + 1)
        + [ANY] * len(sends)
        + [INV] * len(srcs)
        + [HBM] * len(extra),
        out_specs=HBM,
        scratch_shapes=[
            pltpu.VMEM((rows, width), BF16),
            pltpu.VMEM((n - 1, hidden, width), BF16),
            pltpu.SemaphoreType.DMA((len(runs),)),
            pltpu.SemaphoreType.DMA((2 * n - 2,)),
        ],
        input_output_aliases={n + 1 + len(sends) + len(srcs): 0} if last else {},
        compiler_params=limit(5),
        cost_estimate=FREE,
        name=f"proj1_{runs[0][0]}",
    )(*inners, w_proj, *sends, *srcs, *extra)


def on_device(signal, lengths, dilations, w_conv, w_proj, gains, biases):
    own = signal[0]
    rows = own.shape[0]
    width = w_conv.shape[3]
    end = rows - HALO
    n_seq, n = lax.axis_size("seq"), lax.axis_size("chan")
    pairs1 = [(i, i ^ 1) for i in range(n_seq)]
    pairs2 = [(i, i + 1 if i % 2 else i - 1) for i in range(1, n_seq - 1)]
    perm = lax.ppermute
    pinned = pltpu.with_memory_space_constraint
    tied = lax.optimization_barrier

    def others(value):
        return [perm(value, "chan", [(i, (i + k) % n) for i in range(n)]) for k in range(1, n)]

    sent = others(own)
    own = pinned(own, pltpu.HBM)
    taps = [pinned(w, pltpu.VMEM) for w in stage(pinned(w_conv, pltpu.HBM))]
    lengths, dilations = pinned(lengths, pltpu.HBM), pinned(dilations, pltpu.HBM)
    keep = pinned(keeps(lengths, dilations, rows), pltpu.VMEM)
    gains, biases = pinned(gains, pltpu.HBM), pinned(biases, pltpu.HBM)
    own, stat, _, _, gains, biases = pre(own, gains, biases)
    xs = [pinned(own, pltpu.VMEM)] + [pinned(x, pltpu.VMEM) for x in sent]
    found = batch_stats(stat, rows, finish0_kernel, (gains, biases, keep), 1)
    w_proj = pinned(w_proj, pltpu.VMEM)
    vecs = [found[-1]]
    for k in range(1, n):
        pairs = []
        for z in range(n_seq):
            for c in range(n):
                pairs.append((z * n + c, (z ^ 1) * n + (c + k) % n))
        vecs.append(perm(found[-1], ("seq", "chan"), pairs))
    wsend, *wsend1 = cut(w_proj, n, found[-1])
    sent = others(wsend)
    joined, send1, send2 = join(vecs, xs, taps)

    half = rows // 2
    runs = (((HALO, half - HALO),), ((half, half - HALO),), ((0, HALO), (end, HALO)))
    at1, at2 = (5 * HALO, 0), (0, 5 * HALO)

    def inner_rows(layer, chunk, pieces, srcs, stats, *order):
        hand = chunk * (half - HALO)
        return conv(
            pieces,
            srcs,
            n,
            layer,
            runs[chunk],
            dilations,
            stats,
            keep,
            taps[layer],
            width,
            order,
            hand,
        )

    def edge_rows(layer, kept, halos, stats, *order):
        pieces = [(0, 0, 2 * HALO, HALO, None, False), (1, 0, 2 * HALO, 3 * HALO, None, False)]
        srcs = list(kept)
        for halo, at in zip(halos, (at1, at2)):
            pieces += [(len(srcs), 0, HALO, at, None, True)]
            srcs += [halo]
        return conv(
            pieces, srcs, n, layer, runs[2], dilations, stats, keep, taps[layer], width, order
        )[0]

    tall = half + HALO
    pieces_a = [(k, 0, tall, 0, k, True) for k in range(n)]
    pieces_b = [(k, half - HALO, tall, 0, k, True) for k in range(n)]
    inner_a, kept_a = inner_rows(0, 0, pieces_a, xs, joined)
    send1, send2, sent, inner_a = tied((send1, send2, sent, inner_a))
    halos = perm(send1, "seq", pairs1), perm(send2, "seq", pairs2)
    swapped = [perm(w, "groups", SWAP) for w in sent]
    others_a = others(inner_a)
    inner_b, kept_b = inner_rows(0, 1, pieces_b, xs, joined, kept_a)
    swapped, inner_b = tied((swapped, inner_b))
    inner_c = edge_rows(0, (kept_a, kept_b), halos, joined, *others_a)
    sends0 = []
    for w, w2 in zip(sent, swapped):
        sends0 += [w, w2, perm(w, "dp", SWAP), perm(w2, "dp", SWAP)]
    inners = [[inner_a] + others_a] + [[inner] + others(inner) for inner in (inner_b, inner_c)]
    mid, low, high, send1, send2, stat = proj0(runs, inners, w_proj, sends0, xs)
    found = batch_stats(stat, rows, finish1_kernel, (joined,), 0)
    stats1 = found[-1]
    wsend1, _ = tied((wsend1, found[0]))
    sends1 = []
    for k, w in enumerate(wsend1):
        w = perm(w, "chan", [(i, (i + k + 1) % n) for i in range(n)])
        sends1 += [w, perm(w, "dp", SWAP)]
    send1, send2, _ = tied((send1, send2, stats1))
    halos = perm(send1, "seq", pairs1), perm(send2, "seq", pairs2)

    pieces_a = ((0, 0, HALO, 0, None, True), (1, 0, half, HALO, None, True))
    pieces_b = (
        (1, half - 2 * HALO, half, 0, None, True),
        (2, 0, HALO, half, None, True),
    )
    inner_a, kept_a = inner_rows(1, 0, pieces_a, (low, mid), stats1)
    inner_b, kept_b = inner_rows(1, 1, pieces_b, (low, mid, high), stats1, kept_a)
    inner_c = edge_rows(1, (kept_a, kept_b), halos, stats1)
    inners = [[inner] + others(inner) for inner in (inner_a, inner_b, inner_c)]
    out = proj1(((HALO, half - HALO, 0),), rows, inners[0], w_proj, sends1, (mid,))
    out = proj1(((half, half - HALO, half - HALO),), rows, inners[1], w_proj, sends1, (mid,), out)
    ends = ((0, HALO, 0), (end, HALO, 0))
    return proj1(ends, rows, inners[2], w_proj, sends1, (low, high), out)[None]


def solution(mesh):
    placed = (
        P(("groups", "dp"), "seq", "chan"),
        P(("groups", "dp"), None),
        P(),
        P(None, None, None, "chan"),
        P(None, "chan", None),
        P(None, "chan"),
        P(None, "chan"),
    )
    return jax.shard_map(
        on_device,
        mesh=mesh,
        in_specs=placed,
        out_specs=P(("groups", "dp"), "seq", "chan"),
        check_vma=False,
    )
```
